32 devices in a mesh: groups: 2 (over y), cand: 4 (over z), tensor: 4 (over x, core).
Axes of the slice: x: 2, y: 2, z: 4, core: 2. Of those that a mesh axis runs over, the one named last changes fastest.
Arguments:
- tokens: bfloat16 [4096, 4608], P(('groups', 'cand'), 'tensor'), parts along dimension 0, may hold values from -32 to 32
- pre_gain: bfloat16 [1, 4608], P(None, 'tensor'), may hold values from 0.5 to 2
- w_query: bfloat16 [4608, 4096], P(None, 'tensor'), may hold values from -8 to 8
- w_key: bfloat16 [4608, 2048], P(None, 'tensor'), may hold values from -8 to 8
- w_value: bfloat16 [4608, 2048], P(None, 'tensor'), may hold values from -0.09375 to 0.09375
- w_out: bfloat16 [4096, 4608], P('tensor'), may hold values from -8 to 8
- post_gain: bfloat16 [1, 4608], P(None, 'tensor'), may hold values from 0.5 to 2
- cand_lengths: int32 [32], P('groups'), parts along dimension 0, may hold values from 1 to 128, 1536 in all
- pair_mask: int32 [32, 16], P('groups'), parts along dimension 0, may hold values 0 or 1
Outputs:
- update: bfloat16 [4096, 4608], P(('groups', 'cand'), 'tensor'), parts along dimension 0
The draws below stay inside these ranges and needn't reach their ends.
There are 2 independent parts, one for each index of `groups`. The reference program is written for one: setup_inputs(seed, part) draws one part's arguments, and reference() takes and returns one part's arrays. A program takes and returns all parts, laid end to end along the dimension named above; an argument that names none is the same for every part. Nothing has to cross between parts.
Inputs may be any that keep to these rules, and one draw needn't show every extreme that they name: Candidate c holds real tokens at positions 0 to cand_lengths[c] - 1, padding after; some candidate of every prompt has all 128 slots real. `pair_mask`: entry [a, b] says whether candidate a's tokens may attend to candidate b's; a candidate always attends to itself whatever its diagonal entry.
All inputs are finite; a program needn't handle non-finite values.
Results may differ from the reference program's by a relative error of at most 0.012.
Values may be sent and summed in bfloat16 or wider, within the bound.
No kernel may reach another device: no remote copies, remote signals or barrier semaphores. Data moves between devices by JAX's collectives and lax.ppermute only.
A program may use at most 192 MiB of HBM per device.

```python
import math
import jax
import jax.numpy as jnp
import numpy as np
from jax import lax

D = 4608
HEADS = 32
KV_HEADS = 16
HEAD = 128
CTOK = 128
CAND = 16
TOKENS = 2048
N_TENSOR = 4


def draw_tokens(key, part):
    key_base, key_rows = jax.random.split(key, 2)
    column = jnp.arange(D, dtype=jnp.float32) / max(D - 1, 1)
    row_scale = jnp.exp(jax.random.uniform(key_rows, (TOKENS, 1), minval=jnp.log(0.3), maxval=jnp.log(3.0)))
    base = jnp.clip(jax.random.normal(key_base, (TOKENS, D)), -6.0, 6.0)
    col_scale = jnp.exp(0.5 * jnp.log(3.0) * column)
    full = (base * row_scale * col_scale).reshape(CAND, CTOK, D)
    return jnp.clip(full.reshape(TOKENS, D), -32.0, 32.0).astype(jnp.bfloat16)


def query_key_pair(key):
    base_key = jax.random.fold_in(key, 7)
    key_keys, key_queries = jax.random.split(base_key, 2)
    root = jnp.sqrt(jnp.float32(D))
    keys_weight = jnp.clip(jax.random.normal(key_keys, (D, KV_HEADS * HEAD)), -6.0, 6.0) / root
    query_weight = jnp.clip(jax.random.normal(key_queries, (D, HEADS * HEAD)), -6.0, 6.0) / root
    return (jnp.clip(query_weight, -8.0, 8.0), jnp.clip(keys_weight, -8.0, 8.0))


def draw_w_query(key, part):
    return query_key_pair(key)[0].astype(jnp.bfloat16)


def draw_w_key(key, part):
    return query_key_pair(key)[1].astype(jnp.bfloat16)


def draw_w_out(key, part):
    column = jnp.arange(D, dtype=jnp.float32) / max(D - 1, 1)
    col_scale = jnp.exp(0.5 * jnp.log(3.0) * column)
    base = jnp.clip(jax.random.normal(key, (HEADS * HEAD, D)), -6.0, 6.0)
    return jnp.clip(base * col_scale / jnp.sqrt(jnp.float32(HEADS * HEAD)), -8.0, 8.0).astype(jnp.bfloat16)


def with_ends(values, rng, low, high):
    shape = values.shape
    spot = [jax.random.randint(jax.random.fold_in(rng, axis), (), 0, shape[axis]) for axis in range(len(shape))]
    values = values.at[tuple(spot)].set(low)
    longest = shape.index(max(shape))
    spot[longest] = (spot[longest] + 1) % shape[longest]
    return values.at[tuple(spot)].set(high)


def steps_of(stream_key, dims, pieces, low, high):
    gain = 1.0
    for position, parts in pieces:
        steps = jax.random.uniform(jax.random.fold_in(jax.random.fold_in(stream_key, 6), position), (parts,), jnp.float32, low / len(pieces), high / len(pieces))
        gain = gain * jnp.repeat(jnp.exp(steps), dims[position] // parts).reshape((-1,) + (1,) * (len(dims) - 1 - position))
    return gain


def split_up(count, total, limit, slope):
    weights = [(1 << 20) // math.isqrt(rank ** slope) + 1 for rank in range(2, count + 1)]
    rest, given = total - limit - (count - 1), [1] * (count - 1)
    while rest > 0:
        movable = [i for i in range(count - 1) if given[i] < limit]
        whole, budget = sum([weights[i] for i in movable]), rest
        for i in movable:
            addition = min(limit - given[i], max(1, budget * weights[i] // whole), rest)
            given[i] = given[i] + addition
            rest = rest - addition
    return np.array([limit] + given)


def uneven_parts(key, count, total, most, lean):
    if count == 2:
        one = jax.random.randint(key, (), max(1, total - most), min(most, total - 1) + 1)
        return jnp.stack([one, total - one])
    lengths = jnp.asarray(split_up(count, total, most, lean), jnp.int32)
    pairs = (count - 1) // 2
    source_of, sink = lengths[1:1 + 2 * pairs:2], lengths[2:2 + 2 * pairs:2]
    slack = jnp.minimum(source_of - 1, most - sink)
    passed = jax.random.randint(jax.random.fold_in(key, 1), (pairs,), 0, 1 << 20) % (slack + 1)
    lengths = lengths.at[1:1 + 2 * pairs:2].set(source_of - passed).at[2:2 + 2 * pairs:2].set(sink + passed)
    return lengths[jax.random.permutation(jax.random.fold_in(key, 2), count)]


def gaussian(key, extent, deviation, reach, shards=(), kind=jnp.bfloat16):
    drawn = jax.random.normal(key, extent, jnp.float32) * deviation
    if len(shards) > 0:
        drawn = steps_of(key, extent, shards, -0.22, 0.18) * drawn
    return jnp.clip(drawn, min=-reach, max=reach).astype(kind)


def setup_inputs(seed: int = 0, part: int = 0) -> dict:
    streams_of = jax.random.split(jax.random.key(seed), 10)
    own_keys = jax.random.split(jax.random.fold_in(streams_of[9], part), 10)
    return {
        "tokens": draw_tokens(jax.random.fold_in(jax.random.fold_in(streams_of[9], part), 71), part),
        "pre_gain": jnp.clip(jnp.exp(math.log(2.0) - 1.3862944 * jax.random.uniform(streams_of[1], (1, D), jnp.float32) ** steps_of(streams_of[1], (1, D), ((1, 4),), -0.2, 0.2)), 0.5, 2.0).astype(jnp.bfloat16),
        "w_query": draw_w_query(jax.random.fold_in(streams_of[9], 71), part),
        "w_key": draw_w_key(jax.random.fold_in(streams_of[9], 71), part),
        "w_value": gaussian(streams_of[4], (D, KV_HEADS * HEAD), D ** -0.5, 0.09375, ((1, 4),)),
        "w_out": draw_w_out(jax.random.fold_in(streams_of[9], 71), part),
        "post_gain": jnp.clip(jnp.exp(math.log(2.0) - 1.3862944 * jax.random.uniform(streams_of[6], (1, D), jnp.float32) ** steps_of(streams_of[6], (1, D), ((1, 4),), -0.2, 0.2)), 0.5, 2.0).astype(jnp.bfloat16),
        "cand_lengths": uneven_parts(own_keys[7], CAND, CAND * CTOK * 3 // 4, CTOK, 1).astype(jnp.int32),
        "pair_mask": with_ends((jax.random.randint(own_keys[8], (CAND, CAND), 0, 2) < 1).astype(jnp.int32), jax.random.fold_in(own_keys[8], 1), 0, 1),
    }


epsilon = 1e-06

def project_rows(scaled, weight, inverse):
    return (jnp.dot(scaled, weight, preferred_element_type=jnp.float32) * inverse[:, None]).astype(jnp.bfloat16)

def reference(tokens, pre_gain, w_query, w_key, w_value, w_out, post_gain, cand_lengths, pair_mask):
    wide_tokens = tokens.astype(jnp.float32)
    scaled = (wide_tokens * pre_gain.astype(jnp.float32)).astype(jnp.bfloat16)
    inverse = lax.rsqrt(lax.optimization_barrier(jnp.mean(wide_tokens * wide_tokens, axis=1)) + epsilon)
    queries = project_rows(scaled, w_query, inverse)
    keys = project_rows(scaled, w_key, inverse)
    values = project_rows(scaled, w_value, inverse)
    positions = jnp.arange(TOKENS, dtype=jnp.int32)
    cand_of = positions // CTOK
    place_of = positions % CTOK
    paired = pair_mask[cand_of[:, None], cand_of[None, :]] == 1
    allowed = paired | (cand_of[:, None] == cand_of[None, :])
    usable = allowed & (place_of < cand_lengths[cand_of])[None, :]
    head_group = HEADS // KV_HEADS
    score_scale = HEAD ** (-0.5)

    def one_head(head):
        query_cols = lax.dynamic_slice_in_dim(queries, head * HEAD, HEAD, 1)
        kv_start = head // head_group * HEAD
        key_cols = lax.dynamic_slice_in_dim(keys, kv_start, HEAD, 1)
        value_cols = lax.dynamic_slice_in_dim(values, kv_start, HEAD, 1)
        scores = jnp.dot(query_cols, key_cols.T, preferred_element_type=jnp.float32) * score_scale
        scores = jnp.where(usable, scores, -1e+30)
        weights = jnp.exp(scores - lax.optimization_barrier(jnp.max(scores, axis=1, keepdims=True)))
        weights = jnp.where(usable, weights, 0.0)
        numerator = jnp.dot(weights.astype(jnp.bfloat16), value_cols, preferred_element_type=jnp.float32)
        return numerator / lax.optimization_barrier(jnp.sum(weights, axis=1, keepdims=True))
    heads_out = lax.map(one_head, jnp.arange(HEADS, dtype=jnp.int32))
    attended = jnp.transpose(heads_out, (1, 0, 2)).reshape(TOKENS, HEADS * HEAD).astype(jnp.bfloat16)
    block_cols = HEADS * HEAD // N_TENSOR

    def add_block(index, total):
        start = (index * block_cols).astype(jnp.int32)
        left = lax.dynamic_slice_in_dim(attended, start, block_cols, 1)
        right = lax.dynamic_slice_in_dim(w_out, start, block_cols, 0)
        partial_sum = jnp.dot(left, right, preferred_element_type=jnp.float32).astype(jnp.bfloat16)
        partial_sum = lax.optimization_barrier(partial_sum)
        return total + partial_sum.astype(jnp.float32)
    mixed = lax.fori_loop(jnp.int32(0), jnp.int32(N_TENSOR), add_block, jnp.zeros((TOKENS, D), jnp.float32))
    inverse_post = lax.rsqrt(lax.optimization_barrier(jnp.mean(mixed * mixed, axis=1)) + epsilon)
    return (mixed * inverse_post[:, None] * post_gain.astype(jnp.float32)).astype(jnp.bfloat16)
```

```python
import functools
import math

import jax
import jax.numpy as jnp
from jax import lax
from jax.experimental import pallas as pl
from jax.experimental.pallas import tpu as pltpu
from jax.sharding import PartitionSpec as P

HEADS = 32
KV_HEADS = 16
HEAD = 128
CTOK = 128
GROUP = HEADS // KV_HEADS
MASKED = -1e30
EXP2_SCALE = HEAD ** (-0.5) * math.log2(math.e)

epsilon = 1e-06


def bias_rows(cand_lengths, pair_mask, first_cand, cand_local, key_cand):
    allow_rows = lax.dynamic_slice_in_dim(pair_mask, first_cand, cand_local, 0)
    everyone = jnp.arange(pair_mask.shape[1], dtype=jnp.int32)
    one_hot = (everyone[:, None] == key_cand[None, :]).astype(jnp.float32)
    own = first_cand + jnp.arange(cand_local, dtype=jnp.int32)
    allowed = jnp.dot(allow_rows.astype(jnp.float32), one_hot) > 0.5
    allowed = allowed | (own[:, None] == key_cand[None, :])
    lengths = jnp.dot(cand_lengths.astype(jnp.float32)[None, :], one_hot)
    position = jnp.arange(CTOK, dtype=jnp.int32).astype(jnp.float32)
    inside = position[None, :] < lengths[0][:, None]
    usable = allowed[:, :, None] & inside[None]
    return jnp.where(usable, 0.0, MASKED).reshape(cand_local, key_cand.shape[0] * CTOK)


def project_body(rank_ref, *refs, weights):
    x_refs = refs[:4]
    inverse_ref = refs[4]
    w_refs = refs[5 : 5 + 4 * weights]
    out_ref = refs[-1]
    inverse = inverse_ref[...]
    for i in range(weights):
        total = None
        for k in range(4):
            part = jnp.dot(
                x_refs[k][...], w_refs[4 * i + k][...], preferred_element_type=jnp.float32
            )
            total = part if total is None else total + part
        out_ref[i] = (total * inverse).astype(jnp.bfloat16)


def project(rank, blocks, inverse, weights, width):
    rows, features = blocks[0].shape
    columns = weights[0].shape[1]
    in_specs = [pl.BlockSpec((rows, features), lambda j, r: (0, 0)) for _ in range(4)]
    in_specs.append(pl.BlockSpec((rows, 1), lambda j, r: (0, 0)))
    operands = []
    for w in weights:
        for k in range(4):
            in_specs.append(pl.BlockSpec((features, width), lambda j, r, k=k: (r[k], j)))
            operands.append(w)
    return pl.pallas_call(
        functools.partial(project_body, weights=len(weights)),
        grid_spec=pltpu.PrefetchScalarGridSpec(
            num_scalar_prefetch=1,
            grid=(columns // width,),
            in_specs=in_specs,
            out_specs=pl.BlockSpec((len(weights), rows, width), lambda j, r: (0, 0, j)),
        ),
        out_shape=jax.ShapeDtypeStruct((len(weights), rows, columns), jnp.bfloat16),
        compiler_params=pltpu.CompilerParams(vmem_limit_bytes=56 * 2**20),
        name="project",
    )(rank, *blocks, inverse, *operands)


def attention_body(bias_ref, q_ref, *refs, slots):
    kv_refs = refs[: 2 * slots]
    out_ref = refs[2 * slots]
    rows = q_ref.shape[1]
    nt = (((1,), (1,)), ((), ()))
    for c in range(rows // CTOK):
        here = slice(c * CTOK, (c + 1) * CTOK)
        q = jnp.concatenate([q_ref[0, here, g * HEAD : (g + 1) * HEAD] for g in range(GROUP)], axis=0)
        scores = []
        start = 0
        for s in range(slots):
            k = kv_refs[2 * s][0]
            part = lax.dot_general(q, k, nt, preferred_element_type=jnp.float32)
            scores.append(part * EXP2_SCALE + bias_ref[c : c + 1, start : start + k.shape[0]])
            start += k.shape[0]
        top = functools.reduce(jnp.maximum, [jnp.max(s, axis=1, keepdims=True) for s in scores])
        denominator = None
        numerator = None
        for s in range(slots):
            p = jnp.exp2(scores[s] - top)
            d = jnp.sum(p, axis=1, keepdims=True)
            n = jnp.dot(
                p.astype(jnp.bfloat16), kv_refs[2 * s + 1][0], preferred_element_type=jnp.float32
            )
            denominator = d if denominator is None else denominator + d
            numerator = n if numerator is None else numerator + n
        out = (numerator / denominator).astype(jnp.bfloat16)
        for g in range(GROUP):
            out_ref[here, g * HEAD : (g + 1) * HEAD] = out[g * CTOK : (g + 1) * CTOK]


def attention(bias, queries, slots):
    _, rows, width = queries.shape
    heads = width // (GROUP * HEAD)
    in_specs = [
        pl.BlockSpec(bias.shape, lambda h: (0, 0)),
        pl.BlockSpec((1, rows, GROUP * HEAD), lambda h: (0, 0, h)),
    ]
    operands = []
    for kv in slots:
        for i in range(2):
            in_specs.append(pl.BlockSpec((1, kv.shape[1], HEAD), lambda h, i=i: (i, 0, h)))
            operands.append(kv)
    return pl.pallas_call(
        functools.partial(attention_body, slots=len(slots)),
        grid=(heads,),
        in_specs=in_specs,
        out_specs=pl.BlockSpec((rows, GROUP * HEAD), lambda h: (0, h)),
        out_shape=jax.ShapeDtypeStruct((rows, width), jnp.bfloat16),
        compiler_params=pltpu.CompilerParams(vmem_limit_bytes=56 * 2**20),
        name="attention",
    )(bias, queries, *operands)


def output_body(block_ref, x_ref, w_ref, out_ref):
    out_ref[0] = jnp.dot(x_ref[...], w_ref[...], preferred_element_type=jnp.float32).astype(
        jnp.bfloat16
    )


def output_blocks(block_ids, attended, w_out, features):
    rows, inner = attended.shape
    width = features // 3
    return pl.pallas_call(
        output_body,
        grid_spec=pltpu.PrefetchScalarGridSpec(
            num_scalar_prefetch=1,
            grid=(block_ids.shape[0], 3),
            in_specs=[
                pl.BlockSpec((rows, inner), lambda b, j, r: (0, 0)),
                pl.BlockSpec((inner, width), lambda b, j, r: (0, r[b] * 3 + j)),
            ],
            out_specs=pl.BlockSpec((1, rows, width), lambda b, j, r: (b, 0, j)),
        ),
        out_shape=jax.ShapeDtypeStruct((block_ids.shape[0], rows, features), jnp.bfloat16),
        compiler_params=pltpu.CompilerParams(vmem_limit_bytes=56 * 2**20),
        name="output",
    )(block_ids, attended, w_out)


def swap(x, bit):
    return lax.ppermute(x, "tensor", [(t, t ^ bit) for t in range(4)])


def sum_over_tensor(x):
    return x + swap(x, 1) + (swap(x, 2) + swap(x, 3))


CHUNKS = 2
CAND_AXIS = 4


def per_device_4x4(
    tokens, pre_gain, w_query, w_key, w_value, w_out, post_gain, cand_lengths, pair_mask
):
    row_count, features = tokens.shape
    model_width = w_query.shape[0]
    cand_local = row_count // CTOK
    rank = lax.axis_index("tensor").astype(jnp.int32)
    place = lax.axis_index("cand").astype(jnp.int32)
    ranks = jnp.stack([rank, rank ^ 1, rank ^ 2, rank ^ 3])
    step = row_count // CHUNKS

    wide = tokens.astype(jnp.float32)
    scaled = (wide * pre_gain.astype(jnp.float32)).astype(jnp.bfloat16)
    square_sum = sum_over_tensor(jnp.sum(wide * wide, axis=1))
    inverse = lax.rsqrt(square_sum / model_width + epsilon)[:, None]

    blocks = []
    for c in range(CHUNKS):
        own = scaled[c * step : (c + 1) * step]
        far = swap(own, 2)
        blocks.append([own, swap(own, 1), far, swap(far, 1)])

    key_values = []
    for c in range(CHUNKS):
        key_values.append(
            project(ranks, blocks[c], inverse[c * step : (c + 1) * step], [w_key, w_value], 256)
        )
    right = [(i, i + 1) for i in range(CAND_AXIS - 1)]
    left = [(i + 1, i) for i in range(CAND_AXIS - 1)]
    from_left = [key_values]
    from_right = [key_values]
    for s in range(CAND_AXIS - 1):
        from_left.append([lax.ppermute(x, "cand", right) for x in from_left[-1]])
        from_right.append([lax.ppermute(x, "cand", left) for x in from_right[-1]])
    slots = list(key_values)
    shards = [place]
    for s in range(1, CAND_AXIS):
        shards.append((place - s) % CAND_AXIS)
        for c in range(CHUNKS):
            slots.append(jnp.where(place >= s, from_left[s][c], from_right[CAND_AXIS - s][c]))
    key_cand = jnp.concatenate(
        [s * cand_local + jnp.arange(cand_local, dtype=jnp.int32) for s in shards]
    )
    bias = bias_rows(cand_lengths, pair_mask, place * cand_local, cand_local, key_cand)
    queries = [
        project(ranks, blocks[c], inverse[c * step : (c + 1) * step], [w_query], 512)
        for c in range(CHUNKS)
    ]

    gain_wide = post_gain.astype(jnp.float32)
    other_core = jnp.stack([rank ^ 3, rank ^ 1])
    this_core = jnp.stack([rank ^ 2, rank])
    cands = step // CTOK
    updates = []
    for c in range(CHUNKS):
        attended = attention(bias[c * cands : (c + 1) * cands], queries[c], slots)
        away = swap(output_blocks(other_core, attended, w_out, features), 1)
        home = output_blocks(this_core, attended, w_out, features)
        far = (home[0].astype(jnp.float32) + away[0].astype(jnp.float32)).astype(jnp.bfloat16)
        far = swap(far, 2)
        near = home[1].astype(jnp.float32) + away[1].astype(jnp.float32)
        mixed = near + far.astype(jnp.float32)
        mixed_sq = sum_over_tensor(jnp.sum(mixed * mixed, axis=1))
        inverse_post = lax.rsqrt(mixed_sq / model_width + epsilon)
        updates.append((mixed * inverse_post[:, None] * gain_wide).astype(jnp.bfloat16))
    return jnp.concatenate(updates, axis=0)


def per_device(
    tokens, pre_gain, w_query, w_key, w_value, w_out, post_gain, cand_lengths, pair_mask
):
    row_count = tokens.shape[0]
    model_width, query_width = w_query.shape
    kv_width = w_key.shape[1]
    weights_all = jnp.concatenate([w_query, w_key, w_value], axis=1)
    wide = tokens.astype(jnp.float32)
    square_sum = lax.psum(jnp.sum(wide * wide, axis=1), "tensor")
    scaled = (wide * pre_gain.astype(jnp.float32)).astype(jnp.bfloat16)
    scaled = lax.all_gather(scaled, "tensor", axis=1, tiled=True)
    inverse = lax.rsqrt(square_sum / model_width + epsilon)
    projected = jnp.dot(scaled, weights_all, preferred_element_type=jnp.float32)
    projected = (projected * inverse[:, None]).astype(jnp.bfloat16)
    keys = projected[:, query_width : query_width + kv_width]
    values = projected[:, query_width + kv_width :]
    cand_local = row_count // CTOK
    first_cand = lax.axis_index("cand").astype(jnp.int32) * cand_local
    key_cand = jnp.arange(pair_mask.shape[1], dtype=jnp.int32)
    bias = bias_rows(cand_lengths, pair_mask, first_cand, cand_local, key_cand)
    gathered = lax.all_gather(jnp.stack([keys, values]), "cand", axis=1, tiled=True)
    attended = attention(bias, projected[None, :, :query_width], [gathered])
    partial = jnp.dot(attended, w_out, preferred_element_type=jnp.float32).astype(jnp.bfloat16)
    mixed = lax.psum_scatter(partial.T, "tensor", scatter_dimension=0, tiled=True)
    mixed = mixed.astype(jnp.float32).T
    mixed_sq = lax.psum(jnp.sum(mixed * mixed, axis=1), "tensor")
    inverse_post = lax.rsqrt(mixed_sq / model_width + epsilon)
    return (mixed * inverse_post[:, None] * post_gain.astype(jnp.float32)).astype(jnp.bfloat16)


def solution(mesh):
    small = mesh.shape["tensor"] == 4 and mesh.shape["cand"] == CAND_AXIS
    return jax.shard_map(
        per_device_4x4 if small else per_device,
        mesh=mesh,
        in_specs=(
            P(("groups", "cand"), "tensor"),
            P(None, "tensor"),
            P(None, "tensor"),
            P(None, "tensor"),
            P(None, "tensor"),
            P("tensor", None),
            P(None, "tensor"),
            P("groups"),
            P("groups", None),
        ),
        out_specs=P(("groups", "cand"), "tensor"),
        check_vma=False,
    )
```

```python
import functools
import math

import jax
import jax.numpy as jnp
from jax import lax
from jax.experimental import pallas as pl
from jax.experimental.pallas import tpu as pltpu
from jax.sharding import PartitionSpec as P

HEADS = 32
KV_HEADS = 16
HEAD = 128
CTOK = 128
GROUP = HEADS // KV_HEADS
MASKED = -1e30
EXP2_SCALE = HEAD ** (-0.5) * math.log2(math.e)

epsilon = 1e-06


def bias_rows(cand_lengths, pair_mask, first_cand, cand_local, key_cand):
    allow_rows = lax.dynamic_slice_in_dim(pair_mask, first_cand, cand_local, 0)
    everyone = jnp.arange(pair_mask.shape[1], dtype=jnp.int32)
    one_hot = (everyone[:, None] == key_cand[None, :]).astype(jnp.float32)
    own = first_cand + jnp.arange(cand_local, dtype=jnp.int32)
    allowed = jnp.dot(allow_rows.astype(jnp.float32), one_hot) > 0.5
    allowed = allowed | (own[:, None] == key_cand[None, :])
    lengths = jnp.dot(cand_lengths.astype(jnp.float32)[None, :], one_hot)
    position = jnp.arange(CTOK, dtype=jnp.int32).astype(jnp.float32)
    inside = position[None, :] < lengths[0][:, None]
    usable = allowed[:, :, None] & inside[None]
    return jnp.where(usable, 0.0, MASKED).reshape(cand_local, key_cand.shape[0] * CTOK)


def project_body(rank_ref, *refs, weights):
    x_refs = refs[:4]
    inverse_ref = refs[4]
    w_refs = refs[5 : 5 + 4 * weights]
    out_ref = refs[-1]
    inverse = inverse_ref[...]
    for i in range(weights):
        total = None
        for k in range(4):
            part = jnp.dot(
                x_refs[k][...], w_refs[4 * i + k][...], preferred_element_type=jnp.float32
            )
            total = part if total is None else total + part
        out_ref[i] = (total * inverse).astype(jnp.bfloat16)


def project(rank, blocks, inverse, weights, width):
    rows, features = blocks[0].shape
    columns = weights[0].shape[1]
    in_specs = [pl.BlockSpec((rows, features), lambda j, r: (0, 0)) for _ in range(4)]
    in_specs.append(pl.BlockSpec((rows, 1), lambda j, r: (0, 0)))
    operands = []
    for w in weights:
        for k in range(4):
            in_specs.append(pl.BlockSpec((features, width), lambda j, r, k=k: (r[k], j)))
            operands.append(w)
    return pl.pallas_call(
        functools.partial(project_body, weights=len(weights)),
        grid_spec=pltpu.PrefetchScalarGridSpec(
            num_scalar_prefetch=1,
            grid=(columns // width,),
            in_specs=in_specs,
            out_specs=pl.BlockSpec((len(weights), rows, width), lambda j, r: (0, 0, j)),
        ),
        out_shape=jax.ShapeDtypeStruct((len(weights), rows, columns), jnp.bfloat16),
        compiler_params=pltpu.CompilerParams(vmem_limit_bytes=32 * 2**20),
        name="project",
    )(rank, *blocks, inverse, *operands)


def scaled_scores(q, k, bias):
    scores = lax.dot_general(q, k, (((1,), (1,)), ((), ())), preferred_element_type=jnp.float32)
    return scores * EXP2_SCALE + bias


def attention_body(bias_ref, q_ref, *refs, slots, begun, ends):
    kv_refs = refs[: 2 * slots]
    state_refs = refs[2 * slots : 2 * slots + (3 if begun else 0)]
    out_refs = refs[2 * slots + len(state_refs) :]
    rows = q_ref.shape[1]
    for c in range(rows // CTOK):
        here = slice(c * CTOK, (c + 1) * CTOK)

        def stacked(ref):
            return jnp.concatenate(
                [ref[here, g * HEAD : (g + 1) * HEAD] for g in range(GROUP)], axis=0
            )

        q = stacked(q_ref.at[0])
        scores = []
        start = 0
        for s in range(slots):
            k = kv_refs[2 * s][0]
            scores.append(scaled_scores(q, k, bias_ref[c : c + 1, start : start + k.shape[0]]))
            start += k.shape[0]
        top = functools.reduce(jnp.maximum, [jnp.max(s, axis=1, keepdims=True) for s in scores])
        denominator = None
        numerator = None
        if begun:
            old_top = stacked(state_refs[1])
            top = jnp.maximum(old_top[:, :1], top)
            fade = jnp.exp2(old_top - top)
            numerator = stacked(state_refs[0]) * fade
            denominator = stacked(state_refs[2])[:, :1] * fade[:, :1]
        for s in range(slots):
            p = jnp.exp2(scores[s] - top)
            d = jnp.sum(p, axis=1, keepdims=True)
            n = jnp.dot(
                p.astype(jnp.bfloat16), kv_refs[2 * s + 1][0], preferred_element_type=jnp.float32
            )
            denominator = d if denominator is None else denominator + d
            numerator = n if numerator is None else numerator + n
        if ends:
            results = [(numerator / denominator).astype(jnp.bfloat16)]
        else:
            results = [numerator] + [
                jnp.broadcast_to(x, numerator.shape) for x in (top, denominator)
            ]
        for ref, result in zip(out_refs, results):
            for g in range(GROUP):
                ref[here, g * HEAD : (g + 1) * HEAD] = result[g * CTOK : (g + 1) * CTOK]


def attention(bias, queries, slots, state=(), ends=True):
    _, rows, width = queries.shape
    heads = width // (GROUP * HEAD)
    own = pl.BlockSpec((rows, GROUP * HEAD), lambda h: (0, h))
    in_specs = [
        pl.BlockSpec(bias.shape, lambda h: (0, 0)),
        pl.BlockSpec((1, rows, GROUP * HEAD), lambda h: (0, 0, h)),
    ]
    operands = []
    for kv in slots:
        for i in range(2):
            in_specs.append(pl.BlockSpec((1, kv.shape[1], HEAD), lambda h, i=i: (i, 0, h)))
            operands.append(kv)
    if ends:
        out_specs, out_shape = own, jax.ShapeDtypeStruct((rows, width), jnp.bfloat16)
    else:
        out_specs = (own,) * 3
        out_shape = (jax.ShapeDtypeStruct((rows, width), jnp.float32),) * 3
    return pl.pallas_call(
        functools.partial(attention_body, slots=len(slots), begun=len(state) > 0, ends=ends),
        grid=(heads,),
        in_specs=in_specs + [own] * len(state),
        out_specs=out_specs,
        out_shape=out_shape,
        compiler_params=pltpu.CompilerParams(vmem_limit_bytes=40 * 2**20),
        name="attention",
    )(bias, queries, *operands, *state)


def output_body(block_ref, x_ref, w_ref, out_ref):
    width = out_ref.shape[2]
    for b in range(out_ref.shape[0]):
        w = w_ref[:, pl.ds(pl.multiple_of(block_ref[b] * width, HEAD), width)]
        out_ref[b] = jnp.dot(x_ref[...], w, preferred_element_type=jnp.float32).astype(jnp.bfloat16)


def output_blocks(block_ids, attended, w_out, features):
    rows = attended.shape[0]
    return pl.pallas_call(
        output_body,
        in_specs=[
            pl.BlockSpec(memory_space=pltpu.SMEM),
            pl.BlockSpec(memory_space=pltpu.VMEM),
            pl.BlockSpec(memory_space=pltpu.VMEM),
        ],
        out_specs=pl.BlockSpec(memory_space=pltpu.VMEM),
        out_shape=jax.ShapeDtypeStruct((block_ids.shape[0], rows, features), jnp.bfloat16),
        compiler_params=pltpu.CompilerParams(vmem_limit_bytes=24 * 2**20),
        name="output",
    )(block_ids, attended, w_out)


def swap(x, bit):
    return lax.ppermute(x, "tensor", [(t, t ^ bit) for t in range(4)])


def sum_over_tensor(x):
    return x + swap(x, 1) + (swap(x, 2) + swap(x, 3))


TOKEN_CHUNKS = (1, 1, 2)
OUTPUT_CHUNKS = 2
CAND_AXIS = 4


def per_device_4x4(
    tokens, pre_gain, w_query, w_key, w_value, w_out, post_gain, cand_lengths, pair_mask
):
    row_count, features = tokens.shape
    model_width = w_query.shape[0]
    cand_local = row_count // CTOK
    rank = lax.axis_index("tensor").astype(jnp.int32)
    place = lax.axis_index("cand").astype(jnp.int32)
    ranks = jnp.stack([rank, rank ^ 1, rank ^ 2, rank ^ 3])

    wide = tokens.astype(jnp.float32)
    scaled = (wide * pre_gain.astype(jnp.float32)).astype(jnp.bfloat16)
    bounds = [0]
    for share in TOKEN_CHUNKS:
        bounds.append(bounds[-1] + row_count * share // sum(TOKEN_CHUNKS))
    spans = [slice(a, b) for a, b in zip(bounds[:-1], bounds[1:])]

    blocks = []
    for c, span in enumerate(spans):
        own = scaled[span]
        if c == 1:
            own, square_sum = lax.optimization_barrier((own, square_sum))
        far = swap(own, 2)
        if c == 0:
            squares = jnp.sum(wide * wide, axis=1)
            squares, own = lax.optimization_barrier((squares, own))
            square_sum = sum_over_tensor(squares)
        blocks.append([own, swap(own, 1), far, swap(far, 1)])
    inverse = lax.rsqrt(square_sum / model_width + epsilon)[:, None]

    key_values = [
        project(ranks, blocks[c], inverse[span], [w_key, w_value], 256)
        for c, span in enumerate(spans)
    ]
    def outer(parts):
        return [lax.ppermute(x, "cand", [(0, 1), (1, 0), (2, 3), (3, 2)]) for x in parts]

    def inner(parts):
        return [lax.ppermute(x, "cand", [(0, 0), (1, 2), (2, 1), (3, 3)]) for x in parts]

    outer_1 = outer(key_values)
    inner_1 = inner(key_values)
    outer_2 = outer(inner_1)
    inner_2 = inner(outer_1)
    outer_3 = outer(inner_2)
    at_end = (place == 0) | (place == CAND_AXIS - 1)

    def joined(parts, others):
        return jnp.where(at_end, jnp.concatenate(parts, axis=1), jnp.concatenate(others, axis=1))

    slots = [
        jnp.concatenate(key_values, axis=1),
        jnp.concatenate(outer_1, axis=1),
        joined(outer_2, inner_1),
    ]
    last_slot = joined(outer_3, inner_2)
    high = place >= 2
    shards = [
        place,
        place ^ 1,
        jnp.where(high, 1, 2),
        jnp.where(high, 0, 3),
    ]
    key_cand = jnp.concatenate(
        [s * cand_local + jnp.arange(cand_local, dtype=jnp.int32) for s in shards]
    )
    bias = bias_rows(cand_lengths, pair_mask, place * cand_local, cand_local, key_cand)
    queries = jnp.concatenate(
        [
            project(ranks, blocks[c], inverse[span], [w_query], 512)
            for c, span in enumerate(spans)
        ],
        axis=1,
    )
    seen = 3 * row_count
    state = attention(bias[:, :seen], queries, slots, ends=False)
    state, last_slot = lax.optimization_barrier((state, last_slot))

    gain_wide = post_gain.astype(jnp.float32)
    other_core = jnp.stack([rank ^ 3, rank ^ 1])
    this_core = jnp.stack([rank ^ 2, rank])
    step = row_count // OUTPUT_CHUNKS
    cands = step // CTOK
    updates = []
    for c in range(OUTPUT_CHUNKS):
        span = slice(c * step, (c + 1) * step)
        attended = attention(
            bias[c * cands : (c + 1) * cands, seen:],
            queries[:, span],
            [last_slot],
            state=[x[span] for x in state],
        )
        away = swap(output_blocks(other_core, attended, w_out, features), 1)
        home = output_blocks(this_core, attended, w_out, features)
        far = (home[0].astype(jnp.float32) + away[0].astype(jnp.float32)).astype(jnp.bfloat16)
        if c + 1 < OUTPUT_CHUNKS:
            far, last_slot = lax.optimization_barrier((far, last_slot))
        far = swap(far, 2)
        near = home[1].astype(jnp.float32) + away[1].astype(jnp.float32)
        mixed = near + far.astype(jnp.float32)
        mixed_sq = sum_over_tensor(jnp.sum(mixed * mixed, axis=1))
        inverse_post = lax.rsqrt(mixed_sq / model_width + epsilon)
        updates.append((mixed * inverse_post[:, None] * gain_wide).astype(jnp.bfloat16))
    return jnp.concatenate(updates, axis=0)


def per_device(
    tokens, pre_gain, w_query, w_key, w_value, w_out, post_gain, cand_lengths, pair_mask
):
    row_count = tokens.shape[0]
    model_width, query_width = w_query.shape
    kv_width = w_key.shape[1]
    weights_all = jnp.concatenate([w_query, w_key, w_value], axis=1)
    wide = tokens.astype(jnp.float32)
    square_sum = lax.psum(jnp.sum(wide * wide, axis=1), "tensor")
    scaled = (wide * pre_gain.astype(jnp.float32)).astype(jnp.bfloat16)
    scaled = lax.all_gather(scaled, "tensor", axis=1, tiled=True)
    inverse = lax.rsqrt(square_sum / model_width + epsilon)
    projected = jnp.dot(scaled, weights_all, preferred_element_type=jnp.float32)
    projected = (projected * inverse[:, None]).astype(jnp.bfloat16)
    keys = projected[:, query_width : query_width + kv_width]
    values = projected[:, query_width + kv_width :]
    cand_local = row_count // CTOK
    first_cand = lax.axis_index("cand").astype(jnp.int32) * cand_local
    key_cand = jnp.arange(pair_mask.shape[1], dtype=jnp.int32)
    bias = bias_rows(cand_lengths, pair_mask, first_cand, cand_local, key_cand)
    gathered = lax.all_gather(jnp.stack([keys, values]), "cand", axis=1, tiled=True)
    attended = attention(bias, projected[None, :, :query_width], [gathered])
    partial = jnp.dot(attended, w_out, preferred_element_type=jnp.float32).astype(jnp.bfloat16)
    mixed = lax.psum_scatter(partial.T, "tensor", scatter_dimension=0, tiled=True)
    mixed = mixed.astype(jnp.float32).T
    mixed_sq = lax.psum(jnp.sum(mixed * mixed, axis=1), "tensor")
    inverse_post = lax.rsqrt(mixed_sq / model_width + epsilon)
    return (mixed * inverse_post[:, None] * post_gain.astype(jnp.float32)).astype(jnp.bfloat16)


def solution(mesh):
    small = mesh.shape["tensor"] == 4 and mesh.shape["cand"] == CAND_AXIS
    return jax.shard_map(
        per_device_4x4 if small else per_device,
        mesh=mesh,
        in_specs=(
            P(("groups", "cand"), "tensor"),
            P(None, "tensor"),
            P(None, "tensor"),
            P(None, "tensor"),
            P(None, "tensor"),
            P("tensor", None),
            P(None, "tensor"),
            P("groups"),
            P("groups", None),
        ),
        out_specs=P(("groups", "cand"), "tensor"),
        check_vma=False,
    )
```

```python
import functools
import math

import jax
import jax.numpy as jnp
from jax import lax
from jax.experimental import pallas as pl
from jax.experimental.pallas import tpu as pltpu
from jax.sharding import PartitionSpec as P

HEADS = 32
KV_HEADS = 16
HEAD = 128
CTOK = 128
GROUP = HEADS // KV_HEADS
MASKED = -1e30
EXP2_SCALE = HEAD ** (-0.5) * math.log2(math.e)

epsilon = 1e-06


def bias_rows(cand_lengths, pair_mask, first_cand, cand_local, key_cand):
    allow_rows = lax.dynamic_slice_in_dim(pair_mask, first_cand, cand_local, 0)
    everyone = jnp.arange(pair_mask.shape[1], dtype=jnp.int32)
    one_hot = (everyone[:, None] == key_cand[None, :]).astype(jnp.float32)
    own = first_cand + jnp.arange(cand_local, dtype=jnp.int32)
    allowed = jnp.dot(allow_rows.astype(jnp.float32), one_hot) > 0.5
    allowed = allowed | (own[:, None] == key_cand[None, :])
    lengths = jnp.dot(cand_lengths.astype(jnp.float32)[None, :], one_hot)
    position = jnp.arange(CTOK, dtype=jnp.int32).astype(jnp.float32)
    inside = position[None, :] < lengths[0][:, None]
    usable = allowed[:, :, None] & inside[None]
    return jnp.where(usable, 0.0, MASKED).reshape(cand_local, key_cand.shape[0] * CTOK)


LONG = pl.CostEstimate(flops=10**10, transcendentals=0, bytes_accessed=10**6)
SHORT = pl.CostEstimate(flops=1, transcendentals=0, bytes_accessed=1)


def project_body(rank_ref, inverse_ref, *refs, chunks):
    x_refs = refs[: 4 * chunks]
    w_refs = refs[4 * chunks : -1]
    out_ref = refs[-1]
    features = x_refs[0].shape[1]
    start = 0
    for c in range(chunks):
        span = slice(start, start + x_refs[4 * c].shape[0])
        start = span.stop
        for i, w_ref in enumerate(w_refs):
            total = None
            for k in range(4):
                rows = pl.ds(pl.multiple_of(rank_ref[k] * features, HEAD), features)
                part = jnp.dot(
                    x_refs[4 * c + k][...], w_ref[rows, :], preferred_element_type=jnp.float32
                )
                total = part if total is None else total + part
            out_ref[i, span] = (total * inverse_ref[span]).astype(jnp.bfloat16)


def project(ranks, chunks, inverse, weights):
    vmem = pl.BlockSpec(memory_space=pltpu.VMEM)
    blocks = [x for chunk in chunks for x in chunk]
    return pl.pallas_call(
        functools.partial(project_body, chunks=len(chunks)),
        in_specs=[pl.BlockSpec(memory_space=pltpu.SMEM)]
        + [vmem] * (1 + len(blocks) + len(weights)),
        out_specs=vmem,
        out_shape=jax.ShapeDtypeStruct(
            (len(weights), inverse.shape[0], weights[0].shape[1]), jnp.bfloat16
        ),
        compiler_params=pltpu.CompilerParams(vmem_limit_bytes=24 * 2**20),
        cost_estimate=LONG,
        name="project",
    )(ranks, inverse, *blocks, *weights)


def scaled_scores(q, k, bias):
    scores = lax.dot_general(q, k, (((1,), (1,)), ((), ())), preferred_element_type=jnp.float32)
    return scores * EXP2_SCALE + bias


def attention_body(bias_ref, q_ref, *refs, slots, begun, ends):
    kv_refs = refs[: 2 * slots]
    state_refs = refs[2 * slots : 2 * slots + (3 if begun else 0)]
    out_refs = refs[2 * slots + len(state_refs) :]
    rows = q_ref.shape[1]
    for c in range(rows // CTOK):
        here = slice(c * CTOK, (c + 1) * CTOK)

        def stacked(ref):
            return jnp.concatenate(
                [ref[here, g * HEAD : (g + 1) * HEAD] for g in range(GROUP)], axis=0
            )

        q = stacked(q_ref.at[0])
        scores = []
        start = 0
        for s in range(slots):
            k = kv_refs[2 * s][0]
            scores.append(scaled_scores(q, k, bias_ref[c : c + 1, start : start + k.shape[0]]))
            start += k.shape[0]
        top = functools.reduce(jnp.maximum, [jnp.max(s, axis=1, keepdims=True) for s in scores])
        denominator = None
        numerator = None
        if begun:
            old_top = stacked(state_refs[1])
            top = jnp.maximum(old_top[:, :1], top)
            fade = jnp.exp2(old_top - top)
            numerator = stacked(state_refs[0]) * fade
            denominator = stacked(state_refs[2])[:, :1] * fade[:, :1]
        for s in range(slots):
            p = jnp.exp2(scores[s] - top)
            d = jnp.sum(p, axis=1, keepdims=True)
            n = jnp.dot(
                p.astype(jnp.bfloat16), kv_refs[2 * s + 1][0], preferred_element_type=jnp.float32
            )
            denominator = d if denominator is None else denominator + d
            numerator = n if numerator is None else numerator + n
        if ends:
            results = [(numerator / denominator).astype(jnp.bfloat16)]
        else:
            results = [numerator] + [
                jnp.broadcast_to(x, numerator.shape) for x in (top, denominator)
            ]
        for ref, result in zip(out_refs, results):
            for g in range(GROUP):
                ref[here, g * HEAD : (g + 1) * HEAD] = result[g * CTOK : (g + 1) * CTOK]


def attention(bias, queries, slots, state=(), ends=True):
    _, rows, width = queries.shape
    heads = width // (GROUP * HEAD)
    own = pl.BlockSpec((rows, GROUP * HEAD), lambda h: (0, h))
    in_specs = [
        pl.BlockSpec(bias.shape, lambda h: (0, 0)),
        pl.BlockSpec((1, rows, GROUP * HEAD), lambda h: (0, 0, h)),
    ]
    operands = []
    for kv in slots:
        for i in range(2):
            in_specs.append(pl.BlockSpec((1, kv.shape[1], HEAD), lambda h, i=i: (i, 0, h)))
            operands.append(kv)
    if ends:
        out_specs, out_shape = own, jax.ShapeDtypeStruct((rows, width), jnp.bfloat16)
    else:
        out_specs = (own,) * 3
        out_shape = (jax.ShapeDtypeStruct((rows, width), jnp.float32),) * 3
    return pl.pallas_call(
        functools.partial(attention_body, slots=len(slots), begun=len(state) > 0, ends=ends),
        grid=(heads,),
        in_specs=in_specs + [own] * len(state),
        out_specs=out_specs,
        out_shape=out_shape,
        compiler_params=pltpu.CompilerParams(vmem_limit_bytes=20 * 2**20),
        cost_estimate=LONG,
        name="attention",
    )(bias, queries, *operands, *state)


def output_body(block_ref, x_ref, w_ref, out_ref):
    width = out_ref.shape[2]
    for b in range(out_ref.shape[0]):
        w = w_ref[:, pl.ds(pl.multiple_of(block_ref[b] * width, HEAD), width)]
        out_ref[b] = jnp.dot(x_ref[...], w, preferred_element_type=jnp.float32).astype(jnp.bfloat16)


def output_blocks(block_ids, attended, w_out, features):
    rows = attended.shape[0]
    return pl.pallas_call(
        output_body,
        in_specs=[
            pl.BlockSpec(memory_space=pltpu.SMEM),
            pl.BlockSpec(memory_space=pltpu.VMEM),
            pl.BlockSpec(memory_space=pltpu.VMEM),
        ],
        out_specs=pl.BlockSpec(memory_space=pltpu.VMEM),
        out_shape=jax.ShapeDtypeStruct((block_ids.shape[0], rows, features), jnp.bfloat16),
        compiler_params=pltpu.CompilerParams(vmem_limit_bytes=24 * 2**20),
        cost_estimate=SHORT,
        name="output",
    )(block_ids, attended, w_out)


def swap(x, bit):
    return lax.ppermute(x, "tensor", [(t, t ^ bit) for t in range(4)])


def sum_over_tensor(x):
    return x + swap(x, 1) + (swap(x, 2) + swap(x, 3))


TOKEN_CHUNKS = (1, 1, 2)
OUTPUT_CHUNKS = 2
CAND_AXIS = 4


def per_device_4x4(
    tokens, pre_gain, w_query, w_key, w_value, w_out, post_gain, cand_lengths, pair_mask
):
    row_count, features = tokens.shape
    model_width = w_query.shape[0]
    cand_local = row_count // CTOK
    rank = lax.axis_index("tensor").astype(jnp.int32)
    place = lax.axis_index("cand").astype(jnp.int32)
    ranks = jnp.stack([rank, rank ^ 1, rank ^ 2, rank ^ 3])

    wide = tokens.astype(jnp.float32)
    scaled = (wide * pre_gain.astype(jnp.float32)).astype(jnp.bfloat16)
    bounds = [0]
    for share in TOKEN_CHUNKS:
        bounds.append(bounds[-1] + row_count * share // sum(TOKEN_CHUNKS))
    spans = [slice(a, b) for a, b in zip(bounds[:-1], bounds[1:])]

    blocks = []
    for c, span in enumerate(spans):
        own = scaled[span]
        if c == 1:
            own, square_sum = lax.optimization_barrier((own, square_sum))
        if c > 1:
            own, _ = lax.optimization_barrier((own, blocks[c - 2][2]))
        far = swap(own, 2)
        if c == 0:
            squares = jnp.sum(wide * wide, axis=1)
            squares, own = lax.optimization_barrier((squares, own))
            square_sum = sum_over_tensor(squares)
        blocks.append([own, swap(own, 1), far, swap(far, 1)])
    inverse = lax.rsqrt(square_sum / model_width + epsilon)[:, None]

    key_values = []
    for c, span in enumerate(spans):
        if c:
            blocks[c][0], key_values[-1] = lax.optimization_barrier((blocks[c][0], key_values[-1]))
        key_values.append(project(ranks, [blocks[c]], inverse[span], [w_key, w_value]))
    def outer(parts):
        return [lax.ppermute(x, "cand", [(0, 1), (1, 0), (2, 3), (3, 2)]) for x in parts]

    inner_pairs = [(0, 4), (4, 0), (3, 7), (7, 3), (1, 2), (2, 1), (5, 6), (6, 5)]

    def inner(parts):
        return [lax.ppermute(x, ("groups", "cand"), inner_pairs) for x in parts]

    outer_1 = outer(key_values)
    inner_1 = inner(key_values)
    outer_2 = outer(inner_1)
    inner_2 = inner(outer_1)
    outer_3 = outer(inner_2)
    at_end = (place == 0) | (place == CAND_AXIS - 1)

    def joined(parts, others):
        return jnp.where(at_end, jnp.concatenate(parts, axis=1), jnp.concatenate(others, axis=1))

    slots = [
        jnp.concatenate(key_values, axis=1),
        jnp.concatenate(outer_1, axis=1),
        joined(outer_2, inner_1),
    ]
    last_slot = joined(outer_3, inner_2)
    high = place >= 2
    shards = [
        place,
        place ^ 1,
        jnp.where(high, 1, 2),
        jnp.where(high, 0, 3),
    ]
    key_cand = jnp.concatenate(
        [s * cand_local + jnp.arange(cand_local, dtype=jnp.int32) for s in shards]
    )
    bias = bias_rows(cand_lengths, pair_mask, place * cand_local, cand_local, key_cand)
    queries = project(ranks, blocks, inverse, [w_query])
    seen = 3 * row_count
    state = attention(bias[:, :seen], queries, slots, ends=False)
    state, last_slot = lax.optimization_barrier((state, last_slot))

    gain_wide = post_gain.astype(jnp.float32)
    other_core = jnp.stack([rank ^ 3, rank ^ 1])
    this_core = jnp.stack([rank ^ 2, rank])
    step = row_count // OUTPUT_CHUNKS
    cands = step // CTOK
    updates = []
    for c in range(OUTPUT_CHUNKS):
        span = slice(c * step, (c + 1) * step)
        part_bias = bias[c * cands : (c + 1) * cands, seen:]
        part_queries = queries[:, span]
        part_state = [x[span] for x in state]
        attended = attention(part_bias, part_queries, [last_slot], state=part_state)
        away = swap(output_blocks(other_core, attended, w_out, features), 1)
        home = output_blocks(this_core, attended, w_out, features)
        far = (home[0].astype(jnp.float32) + away[0].astype(jnp.float32)).astype(jnp.bfloat16)
        if c + 1 < OUTPUT_CHUNKS:
            far, last_slot = lax.optimization_barrier((far, last_slot))
        far = swap(far, 2)
        near = home[1].astype(jnp.float32) + away[1].astype(jnp.float32)
        mixed = near + far.astype(jnp.float32)
        mixed_sq = sum_over_tensor(jnp.sum(mixed * mixed, axis=1))
        inverse_post = lax.rsqrt(mixed_sq / model_width + epsilon)
        updates.append((mixed * inverse_post[:, None] * gain_wide).astype(jnp.bfloat16))
    return jnp.concatenate(updates, axis=0)


def per_device(
    tokens, pre_gain, w_query, w_key, w_value, w_out, post_gain, cand_lengths, pair_mask
):
    row_count = tokens.shape[0]
    model_width, query_width = w_query.shape
    kv_width = w_key.shape[1]
    weights_all = jnp.concatenate([w_query, w_key, w_value], axis=1)
    wide = tokens.astype(jnp.float32)
    square_sum = lax.psum(jnp.sum(wide * wide, axis=1), "tensor")
    scaled = (wide * pre_gain.astype(jnp.float32)).astype(jnp.bfloat16)
    scaled = lax.all_gather(scaled, "tensor", axis=1, tiled=True)
    inverse = lax.rsqrt(square_sum / model_width + epsilon)
    projected = jnp.dot(scaled, weights_all, preferred_element_type=jnp.float32)
    projected = (projected * inverse[:, None]).astype(jnp.bfloat16)
    keys = projected[:, query_width : query_width + kv_width]
    values = projected[:, query_width + kv_width :]
    cand_local = row_count // CTOK
    first_cand = lax.axis_index("cand").astype(jnp.int32) * cand_local
    key_cand = jnp.arange(pair_mask.shape[1], dtype=jnp.int32)
    bias = bias_rows(cand_lengths, pair_mask, first_cand, cand_local, key_cand)
    gathered = lax.all_gather(jnp.stack([keys, values]), "cand", axis=1, tiled=True)
    attended = attention(bias, projected[None, :, :query_width], [gathered])
    partial = jnp.dot(attended, w_out, preferred_element_type=jnp.float32).astype(jnp.bfloat16)
    mixed = lax.psum_scatter(partial.T, "tensor", scatter_dimension=0, tiled=True)
    mixed = mixed.astype(jnp.float32).T
    mixed_sq = lax.psum(jnp.sum(mixed * mixed, axis=1), "tensor")
    inverse_post = lax.rsqrt(mixed_sq / model_width + epsilon)
    return (mixed * inverse_post[:, None] * post_gain.astype(jnp.float32)).astype(jnp.bfloat16)


def solution(mesh):
    small = mesh.shape["tensor"] == 4 and mesh.shape["cand"] == CAND_AXIS
    small = small and mesh.shape["groups"] == 2
    return jax.shard_map(
        per_device_4x4 if small else per_device,
        mesh=mesh,
        in_specs=(
            P(("groups", "cand"), "tensor"),
            P(None, "tensor"),
            P(None, "tensor"),
            P(None, "tensor"),
            P(None, "tensor"),
            P("tensor", None),
            P(None, "tensor"),
            P("groups"),
            P("groups", None),
        ),
        out_specs=P(("groups", "cand"), "tensor"),
        check_vma=False,
    )
```

```python
import functools
import math

import jax
import jax.numpy as jnp
from jax import lax
from jax.experimental import pallas as pl
from jax.experimental.pallas import tpu as pltpu
from jax.sharding import PartitionSpec as P

HEADS = 32
KV_HEADS = 16
HEAD = 128
CTOK = 128
GROUP = HEADS // KV_HEADS
MASKED = -1e30
EXP2_SCALE = HEAD ** (-0.5) * math.log2(math.e)

epsilon = 1e-06


def bias_rows(cand_lengths, pair_mask, first_cand, cand_local, key_cand):
    allow_rows = lax.dynamic_slice_in_dim(pair_mask, first_cand, cand_local, 0)
    everyone = jnp.arange(pair_mask.shape[1], dtype=jnp.int32)
    one_hot = (everyone[:, None] == key_cand[None, :]).astype(jnp.float32)
    own = first_cand + jnp.arange(cand_local, dtype=jnp.int32)
    allowed = jnp.dot(allow_rows.astype(jnp.float32), one_hot) > 0.5
    allowed = allowed | (own[:, None] == key_cand[None, :])
    lengths = jnp.dot(cand_lengths.astype(jnp.float32)[None, :], one_hot)
    position = jnp.arange(CTOK, dtype=jnp.int32).astype(jnp.float32)
    inside = position[None, :] < lengths[0][:, None]
    usable = allowed[:, :, None] & inside[None]
    return jnp.where(usable, 0.0, MASKED).reshape(cand_local, key_cand.shape[0] * CTOK)


LONG = pl.CostEstimate(flops=10**10, transcendentals=0, bytes_accessed=10**6)
SHORT = pl.CostEstimate(flops=1, transcendentals=0, bytes_accessed=1)


def project_body(rank_ref, inverse_ref, *refs, chunks):
    x_refs = refs[: 4 * chunks]
    w_refs = refs[4 * chunks : -1]
    out_ref = refs[-1]
    features = x_refs[0].shape[1]
    start = 0
    for c in range(chunks):
        span = slice(start, start + x_refs[4 * c].shape[0])
        start = span.stop
        for i, w_ref in enumerate(w_refs):
            total = None
            for k in range(4):
                rows = pl.ds(pl.multiple_of(rank_ref[k] * features, HEAD), features)
                part = jnp.dot(
                    x_refs[4 * c + k][...], w_ref[rows, :], preferred_element_type=jnp.float32
                )
                total = part if total is None else total + part
            out_ref[i, span] = (total * inverse_ref[span]).astype(jnp.bfloat16)


def project(ranks, chunks, inverse, weights):
    vmem = pl.BlockSpec(memory_space=pltpu.VMEM)
    blocks = [x for chunk in chunks for x in chunk]
    return pl.pallas_call(
        functools.partial(project_body, chunks=len(chunks)),
        in_specs=[pl.BlockSpec(memory_space=pltpu.SMEM)]
        + [vmem] * (1 + len(blocks) + len(weights)),
        out_specs=vmem,
        out_shape=jax.ShapeDtypeStruct(
            (len(weights), inverse.shape[0], weights[0].shape[1]), jnp.bfloat16
        ),
        compiler_params=pltpu.CompilerParams(vmem_limit_bytes=24 * 2**20),
        cost_estimate=LONG,
        name="project",
    )(ranks, inverse, *blocks, *weights)


def scaled_scores(q, k, bias):
    scores = lax.dot_general(q, k, (((1,), (1,)), ((), ())), preferred_element_type=jnp.float32)
    return scores * EXP2_SCALE + bias


def attention_body(bias_ref, q_ref, *refs, slots, begun, ends):
    kv_refs = refs[: 2 * slots]
    state_refs = refs[2 * slots : 2 * slots + (2 if begun else 0)]
    out_refs = refs[2 * slots + len(state_refs) :]
    rows = q_ref.shape[1]
    for c in range(rows // CTOK):
        here = slice(c * CTOK, (c + 1) * CTOK)

        def stacked(ref):
            return jnp.concatenate(
                [ref[here, g * HEAD : (g + 1) * HEAD] for g in range(GROUP)], axis=0
            )

        q = stacked(q_ref.at[0])
        scores = []
        start = 0
        for s in range(slots):
            k = kv_refs[2 * s][0]
            scores.append(scaled_scores(q, k, bias_ref[c : c + 1, start : start + k.shape[0]]))
            start += k.shape[0]
        top = functools.reduce(jnp.maximum, [jnp.max(s, axis=1, keepdims=True) for s in scores])
        denominator = None
        numerator = None
        if begun:
            half = HEAD // GROUP
            old = jnp.concatenate(
                [state_refs[1][here, g * half : g * half + 1] for g in range(GROUP)], axis=0
            )
            top = jnp.maximum(old, top)
            denominator = jnp.exp2(old - top)
            numerator = stacked(state_refs[0]) * denominator
        for s in range(slots):
            p = jnp.exp2(scores[s] - top)
            d = jnp.sum(p, axis=1, keepdims=True)
            n = jnp.dot(
                p.astype(jnp.bfloat16), kv_refs[2 * s + 1][0], preferred_element_type=jnp.float32
            )
            denominator = d if denominator is None else denominator + d
            numerator = n if numerator is None else numerator + n
        out = numerator / denominator
        if ends:
            out = out.astype(jnp.bfloat16)
        for g in range(GROUP):
            out_refs[0][here, g * HEAD : (g + 1) * HEAD] = out[g * CTOK : (g + 1) * CTOK]
        if not ends:
            level = top + jnp.log2(denominator)
            half = HEAD // GROUP
            for g in range(GROUP):
                out_refs[1][here, g * half : (g + 1) * half] = jnp.broadcast_to(
                    level[g * CTOK : (g + 1) * CTOK], (CTOK, half)
                )


def attention(bias, queries, slots, state=(), ends=True):
    _, rows, width = queries.shape
    heads = width // (GROUP * HEAD)
    own = pl.BlockSpec((rows, GROUP * HEAD), lambda h: (0, h))
    level = pl.BlockSpec((rows, HEAD), lambda h: (0, h))
    in_specs = [
        pl.BlockSpec(bias.shape, lambda h: (0, 0)),
        pl.BlockSpec((1, rows, GROUP * HEAD), lambda h: (0, 0, h)),
    ]
    operands = []
    for kv in slots:
        for i in range(2):
            in_specs.append(pl.BlockSpec((1, kv.shape[1], HEAD), lambda h, i=i: (i, 0, h)))
            operands.append(kv)
    if ends:
        out_specs, out_shape = own, jax.ShapeDtypeStruct((rows, width), jnp.bfloat16)
    else:
        out_specs = (own, level)
        out_shape = (
            jax.ShapeDtypeStruct((rows, width), jnp.float32),
            jax.ShapeDtypeStruct((rows, heads * HEAD), jnp.float32),
        )
    return pl.pallas_call(
        functools.partial(attention_body, slots=len(slots), begun=len(state) > 0, ends=ends),
        grid=(heads,),
        in_specs=in_specs + ([own, level] if state else []),
        out_specs=out_specs,
        out_shape=out_shape,
        compiler_params=pltpu.CompilerParams(vmem_limit_bytes=20 * 2**20),
        cost_estimate=LONG,
        name="attention",
    )(bias, queries, *operands, *state)


def output_body(block_ref, x_ref, w_ref, out_ref):
    width = out_ref.shape[2]
    for b in range(out_ref.shape[0]):
        w = w_ref[:, pl.ds(pl.multiple_of(block_ref[b] * width, HEAD), width)]
        out_ref[b] = jnp.dot(x_ref[...], w, preferred_element_type=jnp.float32).astype(jnp.bfloat16)


def output_blocks(block_ids, attended, w_out, features):
    rows = attended.shape[0]
    return pl.pallas_call(
        output_body,
        in_specs=[
            pl.BlockSpec(memory_space=pltpu.SMEM),
            pl.BlockSpec(memory_space=pltpu.VMEM),
            pl.BlockSpec(memory_space=pltpu.VMEM),
        ],
        out_specs=pl.BlockSpec(memory_space=pltpu.VMEM),
        out_shape=jax.ShapeDtypeStruct((block_ids.shape[0], rows, features), jnp.bfloat16),
        compiler_params=pltpu.CompilerParams(vmem_limit_bytes=24 * 2**20),
        cost_estimate=SHORT,
        name="output",
    )(block_ids, attended, w_out)


def swap(x, bit):
    return lax.ppermute(x, "tensor", [(t, t ^ bit) for t in range(4)])


def sum_over_tensor(x):
    return x + swap(x, 1) + (swap(x, 2) + swap(x, 3))


TOKEN_CHUNKS = (1, 1, 2)
OUTPUT_CHUNKS = 2
CAND_AXIS = 4


def per_device_4x4(
    tokens, pre_gain, w_query, w_key, w_value, w_out, post_gain, cand_lengths, pair_mask
):
    row_count, features = tokens.shape
    model_width = w_query.shape[0]
    cand_local = row_count // CTOK
    rank = lax.axis_index("tensor").astype(jnp.int32)
    place = lax.axis_index("cand").astype(jnp.int32)
    ranks = jnp.stack([rank, rank ^ 1, rank ^ 2, rank ^ 3])

    wide = tokens.astype(jnp.float32)
    scaled = (wide * pre_gain.astype(jnp.float32)).astype(jnp.bfloat16)
    bounds = [0]
    for share in TOKEN_CHUNKS:
        bounds.append(bounds[-1] + row_count * share // sum(TOKEN_CHUNKS))
    spans = [slice(a, b) for a, b in zip(bounds[:-1], bounds[1:])]

    blocks = []
    for c, span in enumerate(spans):
        own = scaled[span]
        if c == 1:
            own, square_sum = lax.optimization_barrier((own, square_sum))
        if c > 1:
            own, blocks[c - 1][1] = lax.optimization_barrier((own, blocks[c - 1][1]))
        far = swap(own, 2)
        near = swap(own, 1)
        if c == 0:
            squares = jnp.sum(wide * wide, axis=1)
            squares, near = lax.optimization_barrier((squares, near))
            square_sum = sum_over_tensor(squares)
        blocks.append([own, near, far, swap(far, 1)])
    inverse = lax.rsqrt(square_sum / model_width + epsilon)[:, None]

    key_values = []
    for c, span in enumerate(spans):
        if c:
            blocks[c][0], key_values[-1] = lax.optimization_barrier((blocks[c][0], key_values[-1]))
        key_values.append(project(ranks, [blocks[c]], inverse[span], [w_key, w_value]))
    def outer(parts):
        return [lax.ppermute(x, "cand", [(0, 1), (1, 0), (2, 3), (3, 2)]) for x in parts]

    inner_pairs = [(0, 4), (4, 0), (3, 7), (7, 3), (1, 2), (2, 1), (5, 6), (6, 5)]

    def inner(parts):
        return [lax.ppermute(x, ("groups", "cand"), inner_pairs) for x in parts]

    outer_1 = outer(key_values)
    inner_1 = inner(key_values)
    outer_2 = outer(inner_1)
    inner_2 = inner(outer_1)
    outer_3 = outer(inner_2)
    at_end = (place == 0) | (place == CAND_AXIS - 1)

    def joined(parts, others):
        return jnp.where(at_end, jnp.concatenate(parts, axis=1), jnp.concatenate(others, axis=1))

    slots = [
        jnp.concatenate(key_values, axis=1),
        jnp.concatenate(outer_1, axis=1),
        joined(outer_2, inner_1),
    ]
    last_slot = joined(outer_3, inner_2)
    high = place >= 2
    shards = [
        place,
        place ^ 1,
        jnp.where(high, 1, 2),
        jnp.where(high, 0, 3),
    ]
    key_cand = jnp.concatenate(
        [s * cand_local + jnp.arange(cand_local, dtype=jnp.int32) for s in shards]
    )
    bias = bias_rows(cand_lengths, pair_mask, place * cand_local, cand_local, key_cand)
    queries = project(ranks, blocks, inverse, [w_query])
    seen = 3 * row_count
    state = attention(bias[:, :seen], queries, slots, ends=False)
    state, last_slot = lax.optimization_barrier((state, last_slot))

    gain_wide = post_gain.astype(jnp.float32)
    other_core = jnp.stack([rank ^ 3, rank ^ 1])
    this_core = jnp.stack([rank ^ 2, rank])
    step = row_count // OUTPUT_CHUNKS
    attended = attention(bias[:, seen:], queries, [last_slot], state=state)
    pending = []
    for c in range(OUTPUT_CHUNKS):
        rows = attended[c * step : (c + 1) * step]
        if c:
            rows, far = lax.optimization_barrier((rows, pending[-1][2]))
            pending[-1] = (*pending[-1][:2], far)
        away = swap(output_blocks(other_core, rows, w_out, features), 1)
        home = output_blocks(this_core, rows, w_out, features)
        far = (home[0].astype(jnp.float32) + away[0].astype(jnp.float32)).astype(jnp.bfloat16)
        pending.append((home[1], away[1], far))
    pending = [(home, away, swap(far, 2)) for home, away, far in pending]
    updates = []
    for home, away, far in pending:
        near = home.astype(jnp.float32) + away.astype(jnp.float32)
        mixed = near + far.astype(jnp.float32)
        mixed_sq = sum_over_tensor(jnp.sum(mixed * mixed, axis=1))
        inverse_post = lax.rsqrt(mixed_sq / model_width + epsilon)
        updates.append((mixed * inverse_post[:, None] * gain_wide).astype(jnp.bfloat16))
    return jnp.concatenate(updates, axis=0)


def per_device(
    tokens, pre_gain, w_query, w_key, w_value, w_out, post_gain, cand_lengths, pair_mask
):
    row_count = tokens.shape[0]
    model_width, query_width = w_query.shape
    kv_width = w_key.shape[1]
    weights_all = jnp.concatenate([w_query, w_key, w_value], axis=1)
    wide = tokens.astype(jnp.float32)
    square_sum = lax.psum(jnp.sum(wide * wide, axis=1), "tensor")
    scaled = (wide * pre_gain.astype(jnp.float32)).astype(jnp.bfloat16)
    scaled = lax.all_gather(scaled, "tensor", axis=1, tiled=True)
    inverse = lax.rsqrt(square_sum / model_width + epsilon)
    projected = jnp.dot(scaled, weights_all, preferred_element_type=jnp.float32)
    projected = (projected * inverse[:, None]).astype(jnp.bfloat16)
    keys = projected[:, query_width : query_width + kv_width]
    values = projected[:, query_width + kv_width :]
    cand_local = row_count // CTOK
    first_cand = lax.axis_index("cand").astype(jnp.int32) * cand_local
    key_cand = jnp.arange(pair_mask.shape[1], dtype=jnp.int32)
    bias = bias_rows(cand_lengths, pair_mask, first_cand, cand_local, key_cand)
    gathered = lax.all_gather(jnp.stack([keys, values]), "cand", axis=1, tiled=True)
    attended = attention(bias, projected[None, :, :query_width], [gathered])
    partial = jnp.dot(attended, w_out, preferred_element_type=jnp.float32).astype(jnp.bfloat16)
    mixed = lax.psum_scatter(partial.T, "tensor", scatter_dimension=0, tiled=True)
    mixed = mixed.astype(jnp.float32).T
    mixed_sq = lax.psum(jnp.sum(mixed * mixed, axis=1), "tensor")
    inverse_post = lax.rsqrt(mixed_sq / model_width + epsilon)
    return (mixed * inverse_post[:, None] * post_gain.astype(jnp.float32)).astype(jnp.bfloat16)


def solution(mesh):
    small = mesh.shape["tensor"] == 4 and mesh.shape["cand"] == CAND_AXIS
    small = small and mesh.shape["groups"] == 2
    return jax.shard_map(
        per_device_4x4 if small else per_device,
        mesh=mesh,
        in_specs=(
            P(("groups", "cand"), "tensor"),
            P(None, "tensor"),
            P(None, "tensor"),
            P(None, "tensor"),
            P(None, "tensor"),
            P("tensor", None),
            P(None, "tensor"),
            P("groups"),
            P("groups", None),
        ),
        out_specs=P(("groups", "cand"), "tensor"),
        check_vma=False,
    )
```

```python
import functools
import math

import jax
import jax.numpy as jnp
from jax import lax
from jax.experimental import pallas as pl
from jax.experimental.pallas import tpu as pltpu
from jax.sharding import PartitionSpec as P

HEADS = 32
KV_HEADS = 16
HEAD = 128
CTOK = 128
GROUP = HEADS // KV_HEADS
MASKED = -1e30
EXP2_SCALE = HEAD ** (-0.5) * math.log2(math.e)

epsilon = 1e-06


def bias_rows(cand_lengths, pair_mask, first_cand, cand_local, key_cand):
    allow_rows = lax.dynamic_slice_in_dim(pair_mask, first_cand, cand_local, 0)
    everyone = jnp.arange(pair_mask.shape[1], dtype=jnp.int32)
    one_hot = (everyone[:, None] == key_cand[None, :]).astype(jnp.float32)
    own = first_cand + jnp.arange(cand_local, dtype=jnp.int32)
    allowed = jnp.dot(allow_rows.astype(jnp.float32), one_hot) > 0.5
    allowed = allowed | (own[:, None] == key_cand[None, :])
    lengths = jnp.dot(cand_lengths.astype(jnp.float32)[None, :], one_hot)
    position = jnp.arange(CTOK, dtype=jnp.int32).astype(jnp.float32)
    inside = position[None, :] < lengths[0][:, None]
    usable = allowed[:, :, None] & inside[None]
    return jnp.where(usable, 0.0, MASKED).reshape(cand_local, key_cand.shape[0] * CTOK)


LONG = pl.CostEstimate(flops=10**10, transcendentals=0, bytes_accessed=10**6)
SHORT = pl.CostEstimate(flops=1, transcendentals=0, bytes_accessed=1)


def project_body(rank_ref, inverse_ref, *refs, chunks):
    x_refs = refs[: 4 * chunks]
    w_refs = refs[4 * chunks : -1]
    out_ref = refs[-1]
    features = x_refs[0].shape[1]
    start = 0
    for c in range(chunks):
        span = slice(start, start + x_refs[4 * c].shape[0])
        start = span.stop
        for i, w_ref in enumerate(w_refs):
            total = None
            for k in range(4):
                rows = pl.ds(pl.multiple_of(rank_ref[k] * features, HEAD), features)
                part = jnp.dot(
                    x_refs[4 * c + k][...], w_ref[rows, :], preferred_element_type=jnp.float32
                )
                total = part if total is None else total + part
            out_ref[i, span] = (total * inverse_ref[span]).astype(jnp.bfloat16)


def project(ranks, chunks, inverse, weights):
    vmem = pl.BlockSpec(memory_space=pltpu.VMEM)
    blocks = [x for chunk in chunks for x in chunk]
    return pl.pallas_call(
        functools.partial(project_body, chunks=len(chunks)),
        in_specs=[pl.BlockSpec(memory_space=pltpu.SMEM)]
        + [vmem] * (1 + len(blocks) + len(weights)),
        out_specs=vmem,
        out_shape=jax.ShapeDtypeStruct(
            (len(weights), inverse.shape[0], weights[0].shape[1]), jnp.bfloat16
        ),
        compiler_params=pltpu.CompilerParams(vmem_limit_bytes=24 * 2**20),
        cost_estimate=LONG,
        name="project",
    )(ranks, inverse, *blocks, *weights)


def scaled_scores(q, k, bias):
    scores = lax.dot_general(q, k, (((1,), (1,)), ((), ())), preferred_element_type=jnp.float32)
    return scores * EXP2_SCALE + bias


def attention_body(bias_ref, q_ref, *refs, slots, begun, ends):
    kv_refs = refs[: 2 * slots]
    state_refs = refs[2 * slots : 2 * slots + (2 if begun else 0)]
    out_refs = refs[2 * slots + len(state_refs) :]
    rows = q_ref.shape[1]
    for c in range(rows // CTOK):
        here = slice(c * CTOK, (c + 1) * CTOK)

        def stacked(ref):
            return jnp.concatenate(
                [ref[here, g * HEAD : (g + 1) * HEAD] for g in range(GROUP)], axis=0
            )

        q = stacked(q_ref.at[0])
        scores = []
        start = 0
        for s in range(slots):
            k = kv_refs[2 * s][0]
            scores.append(scaled_scores(q, k, bias_ref[c : c + 1, start : start + k.shape[0]]))
            start += k.shape[0]
        top = functools.reduce(jnp.maximum, [jnp.max(s, axis=1, keepdims=True) for s in scores])
        denominator = None
        numerator = None
        if begun:
            half = HEAD // GROUP
            old = jnp.concatenate(
                [state_refs[1][here, g * half : g * half + 1] for g in range(GROUP)], axis=0
            )
            top = jnp.maximum(old, top)
            denominator = jnp.exp2(old - top)
            numerator = stacked(state_refs[0]) * denominator
        for s in range(slots):
            p = jnp.exp2(scores[s] - top)
            d = jnp.sum(p, axis=1, keepdims=True)
            n = jnp.dot(
                p.astype(jnp.bfloat16), kv_refs[2 * s + 1][0], preferred_element_type=jnp.float32
            )
            denominator = d if denominator is None else denominator + d
            numerator = n if numerator is None else numerator + n
        out = numerator / denominator
        if ends:
            out = out.astype(jnp.bfloat16)
        for g in range(GROUP):
            out_refs[0][here, g * HEAD : (g + 1) * HEAD] = out[g * CTOK : (g + 1) * CTOK]
        if not ends:
            level = top + jnp.log2(denominator)
            half = HEAD // GROUP
            for g in range(GROUP):
                out_refs[1][here, g * half : (g + 1) * half] = jnp.broadcast_to(
                    level[g * CTOK : (g + 1) * CTOK], (CTOK, half)
                )


def attention(bias, queries, slots, state=(), ends=True):
    _, rows, width = queries.shape
    heads = width // (GROUP * HEAD)
    own = pl.BlockSpec((rows, GROUP * HEAD), lambda h: (0, h))
    level = pl.BlockSpec((rows, HEAD), lambda h: (0, h))
    in_specs = [
        pl.BlockSpec(bias.shape, lambda h: (0, 0)),
        pl.BlockSpec((1, rows, GROUP * HEAD), lambda h: (0, 0, h)),
    ]
    operands = []
    for kv in slots:
        for i in range(2):
            in_specs.append(pl.BlockSpec((1, kv.shape[1], HEAD), lambda h, i=i: (i, 0, h)))
            operands.append(kv)
    if ends:
        out_specs, out_shape = own, jax.ShapeDtypeStruct((rows, width), jnp.bfloat16)
    else:
        out_specs = (own, level)
        out_shape = (
            jax.ShapeDtypeStruct((rows, width), jnp.float32),
            jax.ShapeDtypeStruct((rows, heads * HEAD), jnp.float32),
        )
    return pl.pallas_call(
        functools.partial(attention_body, slots=len(slots), begun=len(state) > 0, ends=ends),
        grid=(heads,),
        in_specs=in_specs + ([own, level] if state else []),
        out_specs=out_specs,
        out_shape=out_shape,
        compiler_params=pltpu.CompilerParams(vmem_limit_bytes=20 * 2**20),
        cost_estimate=LONG,
        name="attention",
    )(bias, queries, *operands, *state)


def output_body(block_ref, x_ref, w_ref, out_ref):
    width = out_ref.shape[2]
    for b in range(out_ref.shape[0]):
        w = w_ref[:, pl.ds(pl.multiple_of(block_ref[b] * width, HEAD), width)]
        out_ref[b] = jnp.dot(x_ref[...], w, preferred_element_type=jnp.float32).astype(jnp.bfloat16)


def output_blocks(block_ids, attended, w_out, features):
    rows = attended.shape[0]
    return pl.pallas_call(
        output_body,
        in_specs=[
            pl.BlockSpec(memory_space=pltpu.SMEM),
            pl.BlockSpec(memory_space=pltpu.VMEM),
            pl.BlockSpec(memory_space=pltpu.VMEM),
        ],
        out_specs=pl.BlockSpec(memory_space=pltpu.VMEM),
        out_shape=jax.ShapeDtypeStruct((block_ids.shape[0], rows, features), jnp.bfloat16),
        compiler_params=pltpu.CompilerParams(vmem_limit_bytes=24 * 2**20),
        cost_estimate=LONG,
        name="output",
    )(block_ids, attended, w_out)


def swap(x, bit):
    return lax.ppermute(x, "tensor", [(t, t ^ bit) for t in range(4)])


def sum_over_tensor(x):
    return x + swap(x, 1) + (swap(x, 2) + swap(x, 3))


TOKEN_CHUNKS = (1, 1, 2)
OUTPUT_CHUNKS = 2
CAND_AXIS = 4


def per_device_4x4(
    tokens, pre_gain, w_query, w_key, w_value, w_out, post_gain, cand_lengths, pair_mask
):
    row_count, features = tokens.shape
    model_width = w_query.shape[0]
    cand_local = row_count // CTOK
    rank = lax.axis_index("tensor").astype(jnp.int32)
    place = lax.axis_index("cand").astype(jnp.int32)
    ranks = jnp.stack([rank, rank ^ 1, rank ^ 2, rank ^ 3])

    wide = tokens.astype(jnp.float32)
    scaled = (wide * pre_gain.astype(jnp.float32)).astype(jnp.bfloat16)
    bounds = [0]
    for share in TOKEN_CHUNKS:
        bounds.append(bounds[-1] + row_count * share // sum(TOKEN_CHUNKS))
    spans = [slice(a, b) for a, b in zip(bounds[:-1], bounds[1:])]

    blocks = []
    for c, span in enumerate(spans):
        own = scaled[span]
        if c == 1:
            own, square_sum = lax.optimization_barrier((own, square_sum))
        if c > 1:
            own, _ = lax.optimization_barrier((own, blocks[c - 2][2]))
        far = swap(own, 2)
        if c == 0:
            squares = jnp.sum(wide * wide, axis=1)
            squares, own = lax.optimization_barrier((squares, own))
            square_sum = sum_over_tensor(squares)
        blocks.append([own, swap(own, 1), far, swap(far, 1)])
    inverse = lax.rsqrt(square_sum / model_width + epsilon)[:, None]

    key_values = []
    for c, span in enumerate(spans):
        if c:
            blocks[c][0], key_values[-1] = lax.optimization_barrier((blocks[c][0], key_values[-1]))
        key_values.append(project(ranks, [blocks[c]], inverse[span], [w_key, w_value]))
    def outer(parts):
        return [lax.ppermute(x, "cand", [(0, 1), (1, 0), (2, 3), (3, 2)]) for x in parts]

    inner_pairs = [(0, 4), (4, 0), (3, 7), (7, 3), (1, 2), (2, 1), (5, 6), (6, 5)]

    def inner(parts):
        return [lax.ppermute(x, ("groups", "cand"), inner_pairs) for x in parts]

    outer_1 = outer(key_values)
    inner_1 = inner(key_values)
    outer_2 = outer(inner_1)
    inner_2 = inner(outer_1)
    outer_3 = outer(inner_2)
    at_end = (place == 0) | (place == CAND_AXIS - 1)

    def joined(parts, others):
        return jnp.where(at_end, jnp.concatenate(parts, axis=1), jnp.concatenate(others, axis=1))

    slots = [
        jnp.concatenate(key_values, axis=1),
        jnp.concatenate(outer_1, axis=1),
        joined(outer_2, inner_1),
    ]
    last_slot = joined(outer_3, inner_2)
    high = place >= 2
    shards = [
        place,
        place ^ 1,
        jnp.where(high, 1, 2),
        jnp.where(high, 0, 3),
    ]
    key_cand = jnp.concatenate(
        [s * cand_local + jnp.arange(cand_local, dtype=jnp.int32) for s in shards]
    )
    bias = bias_rows(cand_lengths, pair_mask, place * cand_local, cand_local, key_cand)
    queries = project(ranks, blocks, inverse, [w_query])
    seen = 3 * row_count
    state = attention(bias[:, :seen], queries, slots, ends=False)
    state, last_slot = lax.optimization_barrier((state, last_slot))

    gain_wide = post_gain.astype(jnp.float32)
    other_core = jnp.stack([rank ^ 3, rank ^ 1])
    this_core = jnp.stack([rank ^ 2, rank])
    step = row_count // OUTPUT_CHUNKS
    attended = attention(bias[:, seen:], queries, [last_slot], state=state)
    pending = []
    for c in range(OUTPUT_CHUNKS):
        rows = attended[c * step : (c + 1) * step]
        if c:
            rows, far = lax.optimization_barrier((rows, pending[-1][2]))
            pending[-1] = (*pending[-1][:2], far)
        away = swap(output_blocks(other_core, rows, w_out, features), 1)
        home = output_blocks(this_core, rows, w_out, features)
        far = (home[0].astype(jnp.float32) + away[0].astype(jnp.float32)).astype(jnp.bfloat16)
        pending.append((home[1], away[1], far))
    pending = [(home, away, swap(far, 2)) for home, away, far in pending]
    updates = []
    for home, away, far in pending:
        near = home.astype(jnp.float32) + away.astype(jnp.float32)
        mixed = near + far.astype(jnp.float32)
        mixed_sq = sum_over_tensor(jnp.sum(mixed * mixed, axis=1))
        inverse_post = lax.rsqrt(mixed_sq / model_width + epsilon)
        updates.append((mixed * inverse_post[:, None] * gain_wide).astype(jnp.bfloat16))
    return jnp.concatenate(updates, axis=0)


def per_device(
    tokens, pre_gain, w_query, w_key, w_value, w_out, post_gain, cand_lengths, pair_mask
):
    row_count = tokens.shape[0]
    model_width, query_width = w_query.shape
    kv_width = w_key.shape[1]
    weights_all = jnp.concatenate([w_query, w_key, w_value], axis=1)
    wide = tokens.astype(jnp.float32)
    square_sum = lax.psum(jnp.sum(wide * wide, axis=1), "tensor")
    scaled = (wide * pre_gain.astype(jnp.float32)).astype(jnp.bfloat16)
    scaled = lax.all_gather(scaled, "tensor", axis=1, tiled=True)
    inverse = lax.rsqrt(square_sum / model_width + epsilon)
    projected = jnp.dot(scaled, weights_all, preferred_element_type=jnp.float32)
    projected = (projected * inverse[:, None]).astype(jnp.bfloat16)
    keys = projected[:, query_width : query_width + kv_width]
    values = projected[:, query_width + kv_width :]
    cand_local = row_count // CTOK
    first_cand = lax.axis_index("cand").astype(jnp.int32) * cand_local
    key_cand = jnp.arange(pair_mask.shape[1], dtype=jnp.int32)
    bias = bias_rows(cand_lengths, pair_mask, first_cand, cand_local, key_cand)
    gathered = lax.all_gather(jnp.stack([keys, values]), "cand", axis=1, tiled=True)
    attended = attention(bias, projected[None, :, :query_width], [gathered])
    partial = jnp.dot(attended, w_out, preferred_element_type=jnp.float32).astype(jnp.bfloat16)
    mixed = lax.psum_scatter(partial.T, "tensor", scatter_dimension=0, tiled=True)
    mixed = mixed.astype(jnp.float32).T
    mixed_sq = lax.psum(jnp.sum(mixed * mixed, axis=1), "tensor")
    inverse_post = lax.rsqrt(mixed_sq / model_width + epsilon)
    return (mixed * inverse_post[:, None] * post_gain.astype(jnp.float32)).astype(jnp.bfloat16)


def solution(mesh):
    small = mesh.shape["tensor"] == 4 and mesh.shape["cand"] == CAND_AXIS
    small = small and mesh.shape["groups"] == 2
    return jax.shard_map(
        per_device_4x4 if small else per_device,
        mesh=mesh,
        in_specs=(
            P(("groups", "cand"), "tensor"),
            P(None, "tensor"),
            P(None, "tensor"),
            P(None, "tensor"),
            P(None, "tensor"),
            P("tensor", None),
            P(None, "tensor"),
            P("groups"),
            P("groups", None),
        ),
        out_specs=P(("groups", "cand"), "tensor"),
        check_vma=False,
    )
```

```python
import functools
import math

import jax
import jax.numpy as jnp
from jax import lax
from jax.experimental import pallas as pl
from jax.experimental.pallas import tpu as pltpu
from jax.sharding import PartitionSpec as P

HEADS = 32
KV_HEADS = 16
HEAD = 128
CTOK = 128
GROUP = HEADS // KV_HEADS
MASKED = -1e30
EXP2_SCALE = HEAD ** (-0.5) * math.log2(math.e)

epsilon = 1e-06


def bias_rows(cand_lengths, pair_mask, first_cand, cand_local, key_cand):
    allow_rows = lax.dynamic_slice_in_dim(pair_mask, first_cand, cand_local, 0)
    everyone = jnp.arange(pair_mask.shape[1], dtype=jnp.int32)
    one_hot = (everyone[:, None] == key_cand[None, :]).astype(jnp.float32)
    own = first_cand + jnp.arange(cand_local, dtype=jnp.int32)
    allowed = jnp.dot(allow_rows.astype(jnp.float32), one_hot) > 0.5
    allowed = allowed | (own[:, None] == key_cand[None, :])
    lengths = jnp.dot(cand_lengths.astype(jnp.float32)[None, :], one_hot)
    position = jnp.arange(CTOK, dtype=jnp.int32).astype(jnp.float32)
    inside = position[None, :] < lengths[0][:, None]
    usable = allowed[:, :, None] & inside[None]
    return jnp.where(usable, 0.0, MASKED).reshape(cand_local, key_cand.shape[0] * CTOK)


LONG = pl.CostEstimate(flops=10**10, transcendentals=0, bytes_accessed=10**6)
SHORT = pl.CostEstimate(flops=1, transcendentals=0, bytes_accessed=1)


def project_body(rank_ref, inverse_ref, *refs, chunks):
    x_refs = refs[: 4 * chunks]
    w_refs = refs[4 * chunks : -1]
    out_ref = refs[-1]
    features = x_refs[0].shape[1]
    start = 0
    for c in range(chunks):
        span = slice(start, start + x_refs[4 * c].shape[0])
        start = span.stop
        for i, w_ref in enumerate(w_refs):
            total = None
            for k in range(4):
                rows = pl.ds(pl.multiple_of(rank_ref[k] * features, HEAD), features)
                part = jnp.dot(
                    x_refs[4 * c + k][...], w_ref[rows, :], preferred_element_type=jnp.float32
                )
                total = part if total is None else total + part
            out_ref[i, span] = (total * inverse_ref[span]).astype(jnp.bfloat16)


def project(ranks, chunks, inverse, weights):
    vmem = pl.BlockSpec(memory_space=pltpu.VMEM)
    blocks = [x for chunk in chunks for x in chunk]
    return pl.pallas_call(
        functools.partial(project_body, chunks=len(chunks)),
        in_specs=[pl.BlockSpec(memory_space=pltpu.SMEM)]
        + [vmem] * (1 + len(blocks) + len(weights)),
        out_specs=vmem,
        out_shape=jax.ShapeDtypeStruct(
            (len(weights), inverse.shape[0], weights[0].shape[1]), jnp.bfloat16
        ),
        compiler_params=pltpu.CompilerParams(vmem_limit_bytes=24 * 2**20),
        cost_estimate=LONG,
        name="project",
    )(ranks, inverse, *blocks, *weights)


def scaled_scores(q, k, bias):
    scores = lax.dot_general(q, k, (((1,), (1,)), ((), ())), preferred_element_type=jnp.float32)
    return scores * EXP2_SCALE + bias


def attention_body(bias_ref, q_ref, *refs, slots, begun, ends):
    kv_refs = refs[: 2 * slots]
    state_refs = refs[2 * slots : 2 * slots + (2 if begun else 0)]
    out_refs = refs[2 * slots + len(state_refs) :]
    rows = q_ref.shape[1]
    for c in range(rows // CTOK):
        here = slice(c * CTOK, (c + 1) * CTOK)

        def stacked(ref):
            return jnp.concatenate(
                [ref[here, g * HEAD : (g + 1) * HEAD] for g in range(GROUP)], axis=0
            )

        q = stacked(q_ref.at[0])
        scores = []
        start = 0
        for s in range(slots):
            k = kv_refs[2 * s][0]
            scores.append(scaled_scores(q, k, bias_ref[c : c + 1, start : start + k.shape[0]]))
            start += k.shape[0]
        top = functools.reduce(jnp.maximum, [jnp.max(s, axis=1, keepdims=True) for s in scores])
        denominator = None
        numerator = None
        if begun:
            half = HEAD // GROUP
            old = jnp.concatenate(
                [state_refs[1][here, g * half : g * half + 1] for g in range(GROUP)], axis=0
            )
            top = jnp.maximum(old, top)
            denominator = jnp.exp2(old - top)
            numerator = stacked(state_refs[0]) * denominator
        for s in range(slots):
            p = jnp.exp2(scores[s] - top)
            d = jnp.sum(p, axis=1, keepdims=True)
            n = jnp.dot(
                p.astype(jnp.bfloat16), kv_refs[2 * s + 1][0], preferred_element_type=jnp.float32
            )
            denominator = d if denominator is None else denominator + d
            numerator = n if numerator is None else numerator + n
        out = numerator / denominator
        if ends:
            out = out.astype(jnp.bfloat16)
        for g in range(GROUP):
            out_refs[0][here, g * HEAD : (g + 1) * HEAD] = out[g * CTOK : (g + 1) * CTOK]
        if not ends:
            level = top + jnp.log2(denominator)
            half = HEAD // GROUP
            for g in range(GROUP):
                out_refs[1][here, g * half : (g + 1) * half] = jnp.broadcast_to(
                    level[g * CTOK : (g + 1) * CTOK], (CTOK, half)
                )


def attention(bias, queries, slots, state=(), ends=True):
    _, rows, width = queries.shape
    heads = width // (GROUP * HEAD)
    own = pl.BlockSpec((rows, GROUP * HEAD), lambda h: (0, h))
    level = pl.BlockSpec((rows, HEAD), lambda h: (0, h))
    in_specs = [
        pl.BlockSpec(bias.shape, lambda h: (0, 0)),
        pl.BlockSpec((1, rows, GROUP * HEAD), lambda h: (0, 0, h)),
    ]
    operands = []
    for kv in slots:
        for i in range(2):
            in_specs.append(pl.BlockSpec((1, kv.shape[1], HEAD), lambda h, i=i: (i, 0, h)))
            operands.append(kv)
    if ends:
        out_specs, out_shape = own, jax.ShapeDtypeStruct((rows, width), jnp.bfloat16)
    else:
        out_specs = (own, level)
        out_shape = (
            jax.ShapeDtypeStruct((rows, width), jnp.float32),
            jax.ShapeDtypeStruct((rows, heads * HEAD), jnp.float32),
        )
    return pl.pallas_call(
        functools.partial(attention_body, slots=len(slots), begun=len(state) > 0, ends=ends),
        grid=(heads,),
        in_specs=in_specs + ([own, level] if state else []),
        out_specs=out_specs,
        out_shape=out_shape,
        compiler_params=pltpu.CompilerParams(vmem_limit_bytes=20 * 2**20),
        cost_estimate=LONG,
        name="attention",
    )(bias, queries, *operands, *state)


def output_body(block_ref, x_ref, w_ref, out_ref):
    width = out_ref.shape[2]
    for b in range(out_ref.shape[0]):
        w = w_ref[:, pl.ds(pl.multiple_of(block_ref[b] * width, HEAD), width)]
        out_ref[b] = jnp.dot(x_ref[...], w, preferred_element_type=jnp.float32).astype(jnp.bfloat16)


def output_blocks(block_ids, attended, w_out, features):
    rows = attended.shape[0]
    return pl.pallas_call(
        output_body,
        in_specs=[
            pl.BlockSpec(memory_space=pltpu.SMEM),
            pl.BlockSpec(memory_space=pltpu.VMEM),
            pl.BlockSpec(memory_space=pltpu.VMEM),
        ],
        out_specs=pl.BlockSpec(memory_space=pltpu.VMEM),
        out_shape=jax.ShapeDtypeStruct((block_ids.shape[0], rows, features), jnp.bfloat16),
        compiler_params=pltpu.CompilerParams(vmem_limit_bytes=24 * 2**20),
        cost_estimate=LONG,
        name="output",
    )(block_ids, attended, w_out)


def swap(x, bit):
    return lax.ppermute(x, "tensor", [(t, t ^ bit) for t in range(4)])


def sum_over_tensor(x):
    return x + swap(x, 1) + (swap(x, 2) + swap(x, 3))


TOKEN_CHUNKS = (1, 1, 2)
OUTPUT_CHUNKS = 2
CAND_AXIS = 4


def per_device_4x4(
    tokens, pre_gain, w_query, w_key, w_value, w_out, post_gain, cand_lengths, pair_mask
):
    row_count, features = tokens.shape
    model_width = w_query.shape[0]
    cand_local = row_count // CTOK
    rank = lax.axis_index("tensor").astype(jnp.int32)
    place = lax.axis_index("cand").astype(jnp.int32)
    ranks = jnp.stack([rank, rank ^ 1, rank ^ 2, rank ^ 3])

    wide = tokens.astype(jnp.float32)
    scaled = (wide * pre_gain.astype(jnp.float32)).astype(jnp.bfloat16)
    bounds = [0]
    for share in TOKEN_CHUNKS:
        bounds.append(bounds[-1] + row_count * share // sum(TOKEN_CHUNKS))
    spans = [slice(a, b) for a, b in zip(bounds[:-1], bounds[1:])]

    blocks = []
    for c, span in enumerate(spans):
        own = scaled[span]
        if c == 1:
            own, square_sum = lax.optimization_barrier((own, square_sum))
        if c > 1:
            own, _ = lax.optimization_barrier((own, blocks[c - 2][2]))
        far = swap(own, 2)
        if c == 0:
            squares = jnp.sum(wide * wide, axis=1)
            squares, own = lax.optimization_barrier((squares, own))
            square_sum = sum_over_tensor(squares)
        blocks.append([own, swap(own, 1), far, swap(far, 1)])
    inverse = lax.rsqrt(square_sum / model_width + epsilon)[:, None]

    key_values = []
    for c, span in enumerate(spans):
        if c:
            blocks[c][0], key_values[-1] = lax.optimization_barrier((blocks[c][0], key_values[-1]))
        key_values.append(project(ranks, [blocks[c]], inverse[span], [w_key, w_value]))
    def outer(parts):
        return [lax.ppermute(x, "cand", [(0, 1), (1, 0), (2, 3), (3, 2)]) for x in parts]

    inner_pairs = [(0, 4), (4, 0), (3, 7), (7, 3), (1, 2), (2, 1), (5, 6), (6, 5)]

    def inner(parts):
        return [lax.ppermute(x, ("groups", "cand"), inner_pairs) for x in parts]

    outer_1 = outer(key_values)
    inner_1 = inner(key_values)
    outer_2 = outer(inner_1)
    inner_2 = inner(outer_1)
    outer_3 = outer(inner_2)
    at_end = (place == 0) | (place == CAND_AXIS - 1)

    def joined(parts, others):
        return jnp.where(at_end, jnp.concatenate(parts, axis=1), jnp.concatenate(others, axis=1))

    slots = [
        jnp.concatenate(key_values, axis=1),
        jnp.concatenate(outer_1, axis=1),
        joined(outer_2, inner_1),
    ]
    last_slot = joined(outer_3, inner_2)
    high = place >= 2
    shards = [
        place,
        place ^ 1,
        jnp.where(high, 1, 2),
        jnp.where(high, 0, 3),
    ]
    key_cand = jnp.concatenate(
        [s * cand_local + jnp.arange(cand_local, dtype=jnp.int32) for s in shards]
    )
    bias = bias_rows(cand_lengths, pair_mask, place * cand_local, cand_local, key_cand)
    queries = project(ranks, blocks, inverse, [w_query])
    seen = 3 * row_count
    state = attention(bias[:, :seen], queries, slots, ends=False)
    state, last_slot = lax.optimization_barrier((state, last_slot))

    gain_wide = post_gain.astype(jnp.float32)
    other_core = jnp.stack([rank ^ 3, rank ^ 1])
    this_core = jnp.stack([rank ^ 2, rank])
    step = row_count // OUTPUT_CHUNKS
    cands = step // CTOK
    pending = []
    for c in range(OUTPUT_CHUNKS):
        span = slice(c * step, (c + 1) * step)
        if c:
            last_slot, far = lax.optimization_barrier((last_slot, pending[-1][2]))
            pending[-1] = (*pending[-1][:2], far)
        rows = attention(
            bias[c * cands : (c + 1) * cands, seen:],
            queries[:, span],
            [last_slot],
            state=[x[span] for x in state],
        )
        away = swap(output_blocks(other_core, rows, w_out, features), 1)
        home = output_blocks(this_core, rows, w_out, features)
        far = (home[0].astype(jnp.float32) + away[0].astype(jnp.float32)).astype(jnp.bfloat16)
        pending.append((home[1], away[1], far))
    pending = [(home, away, swap(far, 2)) for home, away, far in pending]
    updates = []
    for home, away, far in pending:
        near = home.astype(jnp.float32) + away.astype(jnp.float32)
        mixed = near + far.astype(jnp.float32)
        mixed_sq = sum_over_tensor(jnp.sum(mixed * mixed, axis=1))
        inverse_post = lax.rsqrt(mixed_sq / model_width + epsilon)
        updates.append((mixed * inverse_post[:, None] * gain_wide).astype(jnp.bfloat16))
    return jnp.concatenate(updates, axis=0)


def per_device(
    tokens, pre_gain, w_query, w_key, w_value, w_out, post_gain, cand_lengths, pair_mask
):
    row_count = tokens.shape[0]
    model_width, query_width = w_query.shape
    kv_width = w_key.shape[1]
    weights_all = jnp.concatenate([w_query, w_key, w_value], axis=1)
    wide = tokens.astype(jnp.float32)
    square_sum = lax.psum(jnp.sum(wide * wide, axis=1), "tensor")
    scaled = (wide * pre_gain.astype(jnp.float32)).astype(jnp.bfloat16)
    scaled = lax.all_gather(scaled, "tensor", axis=1, tiled=True)
    inverse = lax.rsqrt(square_sum / model_width + epsilon)
    projected = jnp.dot(scaled, weights_all, preferred_element_type=jnp.float32)
    projected = (projected * inverse[:, None]).astype(jnp.bfloat16)
    keys = projected[:, query_width : query_width + kv_width]
    values = projected[:, query_width + kv_width :]
    cand_local = row_count // CTOK
    first_cand = lax.axis_index("cand").astype(jnp.int32) * cand_local
    key_cand = jnp.arange(pair_mask.shape[1], dtype=jnp.int32)
    bias = bias_rows(cand_lengths, pair_mask, first_cand, cand_local, key_cand)
    gathered = lax.all_gather(jnp.stack([keys, values]), "cand", axis=1, tiled=True)
    attended = attention(bias, projected[None, :, :query_width], [gathered])
    partial = jnp.dot(attended, w_out, preferred_element_type=jnp.float32).astype(jnp.bfloat16)
    mixed = lax.psum_scatter(partial.T, "tensor", scatter_dimension=0, tiled=True)
    mixed = mixed.astype(jnp.float32).T
    mixed_sq = lax.psum(jnp.sum(mixed * mixed, axis=1), "tensor")
    inverse_post = lax.rsqrt(mixed_sq / model_width + epsilon)
    return (mixed * inverse_post[:, None] * post_gain.astype(jnp.float32)).astype(jnp.bfloat16)


def solution(mesh):
    small = mesh.shape["tensor"] == 4 and mesh.shape["cand"] == CAND_AXIS
    small = small and mesh.shape["groups"] == 2
    return jax.shard_map(
        per_device_4x4 if small else per_device,
        mesh=mesh,
        in_specs=(
            P(("groups", "cand"), "tensor"),
            P(None, "tensor"),
            P(None, "tensor"),
            P(None, "tensor"),
            P(None, "tensor"),
            P("tensor", None),
            P(None, "tensor"),
            P("groups"),
            P("groups", None),
        ),
        out_specs=P(("groups", "cand"), "tensor"),
        check_vma=False,
    )
```

```python
import functools
import math

import jax
import jax.numpy as jnp
from jax import lax
from jax.experimental import pallas as pl
from jax.experimental.pallas import tpu as pltpu
from jax.sharding import PartitionSpec as P

HEADS = 32
KV_HEADS = 16
HEAD = 128
CTOK = 128
GROUP = HEADS // KV_HEADS
MASKED = -1e30
EXP2_SCALE = HEAD ** (-0.5) * math.log2(math.e)

epsilon = 1e-06


def bias_rows(cand_lengths, pair_mask, first_cand, cand_local, key_cand):
    allow_rows = lax.dynamic_slice_in_dim(pair_mask, first_cand, cand_local, 0)
    everyone = jnp.arange(pair_mask.shape[1], dtype=jnp.int32)
    one_hot = (everyone[:, None] == key_cand[None, :]).astype(jnp.float32)
    own = first_cand + jnp.arange(cand_local, dtype=jnp.int32)
    allowed = jnp.dot(allow_rows.astype(jnp.float32), one_hot) > 0.5
    allowed = allowed | (own[:, None] == key_cand[None, :])
    lengths = jnp.dot(cand_lengths.astype(jnp.float32)[None, :], one_hot)
    position = jnp.arange(CTOK, dtype=jnp.int32).astype(jnp.float32)
    inside = position[None, :] < lengths[0][:, None]
    usable = allowed[:, :, None] & inside[None]
    return jnp.where(usable, 0.0, MASKED).reshape(cand_local, key_cand.shape[0] * CTOK)


LONG = pl.CostEstimate(flops=10**10, transcendentals=0, bytes_accessed=10**6)
SHORT = pl.CostEstimate(flops=1, transcendentals=0, bytes_accessed=1)


def project_body(rank_ref, inverse_ref, after_ref, *refs, chunks):
    x_refs = refs[: 4 * chunks]
    w_refs = refs[4 * chunks : -2]
    out_ref, mark_ref = refs[-2:]
    mark_ref[...] = after_ref[...]
    features = x_refs[0].shape[1]
    start = 0
    for c in range(chunks):
        span = slice(start, start + x_refs[4 * c].shape[0])
        start = span.stop
        for i, w_ref in enumerate(w_refs):
            total = None
            for k in range(4):
                rows = pl.ds(pl.multiple_of(rank_ref[k] * features, HEAD), features)
                part = jnp.dot(
                    x_refs[4 * c + k][...], w_ref[rows, :], preferred_element_type=jnp.float32
                )
                total = part if total is None else total + part
            out_ref[i, span] = (total * inverse_ref[span]).astype(jnp.bfloat16)


def project(ranks, after, chunks, inverse, weights):
    vmem = pl.BlockSpec(memory_space=pltpu.VMEM)
    blocks = [x for chunk in chunks for x in chunk]
    return pl.pallas_call(
        functools.partial(project_body, chunks=len(chunks)),
        in_specs=[pl.BlockSpec(memory_space=pltpu.SMEM)]
        + [vmem] * (2 + len(blocks) + len(weights)),
        out_specs=(vmem, vmem),
        out_shape=(
            jax.ShapeDtypeStruct(
                (len(weights), inverse.shape[0], weights[0].shape[1]), jnp.bfloat16
            ),
            jax.ShapeDtypeStruct(after.shape, after.dtype),
        ),
        compiler_params=pltpu.CompilerParams(vmem_limit_bytes=24 * 2**20),
        cost_estimate=LONG,
        name="project",
    )(ranks, inverse, after, *blocks, *weights)


def scaled_scores(q, k, bias):
    scores = lax.dot_general(q, k, (((1,), (1,)), ((), ())), preferred_element_type=jnp.float32)
    return scores * EXP2_SCALE + bias


def attention_body(bias_ref, q_ref, *refs, slots, begun, ends):
    kv_refs = refs[: 2 * slots]
    state_refs = refs[2 * slots : 2 * slots + (2 if begun else 0)]
    out_refs = refs[2 * slots + len(state_refs) :]
    rows = q_ref.shape[1]
    for c in range(rows // CTOK):
        here = slice(c * CTOK, (c + 1) * CTOK)

        def stacked(ref):
            return jnp.concatenate(
                [ref[here, g * HEAD : (g + 1) * HEAD] for g in range(GROUP)], axis=0
            )

        q = stacked(q_ref.at[0])
        scores = []
        start = 0
        for s in range(slots):
            k = kv_refs[2 * s][0]
            scores.append(scaled_scores(q, k, bias_ref[c : c + 1, start : start + k.shape[0]]))
            start += k.shape[0]
        top = functools.reduce(jnp.maximum, [jnp.max(s, axis=1, keepdims=True) for s in scores])
        denominator = None
        numerator = None
        if begun:
            half = HEAD // GROUP
            old = jnp.concatenate(
                [state_refs[1][here, g * half : g * half + 1] for g in range(GROUP)], axis=0
            )
            top = jnp.maximum(old, top)
            denominator = jnp.exp2(old - top)
            numerator = stacked(state_refs[0]) * denominator
        for s in range(slots):
            p = jnp.exp2(scores[s] - top)
            d = jnp.sum(p, axis=1, keepdims=True)
            n = jnp.dot(
                p.astype(jnp.bfloat16), kv_refs[2 * s + 1][0], preferred_element_type=jnp.float32
            )
            denominator = d if denominator is None else denominator + d
            numerator = n if numerator is None else numerator + n
        out = numerator / denominator
        if ends:
            out = out.astype(jnp.bfloat16)
        for g in range(GROUP):
            out_refs[0][here, g * HEAD : (g + 1) * HEAD] = out[g * CTOK : (g + 1) * CTOK]
        if not ends:
            level = top + jnp.log2(denominator)
            half = HEAD // GROUP
            for g in range(GROUP):
                out_refs[1][here, g * half : (g + 1) * half] = jnp.broadcast_to(
                    level[g * CTOK : (g + 1) * CTOK], (CTOK, half)
                )


def attention(bias, queries, slots, state=(), ends=True):
    _, rows, width = queries.shape
    heads = width // (GROUP * HEAD)
    own = pl.BlockSpec((rows, GROUP * HEAD), lambda h: (0, h))
    level = pl.BlockSpec((rows, HEAD), lambda h: (0, h))
    in_specs = [
        pl.BlockSpec(bias.shape, lambda h: (0, 0)),
        pl.BlockSpec((1, rows, GROUP * HEAD), lambda h: (0, 0, h)),
    ]
    operands = []
    for kv in slots:
        for i in range(2):
            in_specs.append(pl.BlockSpec((1, kv.shape[1], HEAD), lambda h, i=i: (i, 0, h)))
            operands.append(kv)
    if ends:
        out_specs, out_shape = own, jax.ShapeDtypeStruct((rows, width), jnp.bfloat16)
    else:
        out_specs = (own, level)
        out_shape = (
            jax.ShapeDtypeStruct((rows, width), jnp.float32),
            jax.ShapeDtypeStruct((rows, heads * HEAD), jnp.float32),
        )
    return pl.pallas_call(
        functools.partial(attention_body, slots=len(slots), begun=len(state) > 0, ends=ends),
        grid=(heads,),
        in_specs=in_specs + ([own, level] if state else []),
        out_specs=out_specs,
        out_shape=out_shape,
        compiler_params=pltpu.CompilerParams(vmem_limit_bytes=20 * 2**20),
        cost_estimate=LONG,
        name="attention",
    )(bias, queries, *operands, *state)


def output_body(block_ref, x_ref, w_ref, out_ref):
    width = out_ref.shape[2]
    for b in range(out_ref.shape[0]):
        w = w_ref[:, pl.ds(pl.multiple_of(block_ref[b] * width, HEAD), width)]
        out_ref[b] = jnp.dot(x_ref[...], w, preferred_element_type=jnp.float32).astype(jnp.bfloat16)


def output_blocks(block_ids, attended, w_out, features):
    rows = attended.shape[0]
    return pl.pallas_call(
        output_body,
        in_specs=[
            pl.BlockSpec(memory_space=pltpu.SMEM),
            pl.BlockSpec(memory_space=pltpu.VMEM),
            pl.BlockSpec(memory_space=pltpu.VMEM),
        ],
        out_specs=pl.BlockSpec(memory_space=pltpu.VMEM),
        out_shape=jax.ShapeDtypeStruct((block_ids.shape[0], rows, features), jnp.bfloat16),
        compiler_params=pltpu.CompilerParams(vmem_limit_bytes=24 * 2**20),
        cost_estimate=LONG,
        name="output",
    )(block_ids, attended, w_out)


def swap(x, bit):
    return lax.ppermute(x, "tensor", [(t, t ^ bit) for t in range(4)])


def sum_over_tensor(x):
    return x + swap(x, 1) + (swap(x, 2) + swap(x, 3))


TOKEN_CHUNKS = (1, 1, 2)
OUTPUT_CHUNKS = 2
CAND_AXIS = 4


def per_device_4x4(
    tokens, pre_gain, w_query, w_key, w_value, w_out, post_gain, cand_lengths, pair_mask
):
    row_count, features = tokens.shape
    model_width = w_query.shape[0]
    cand_local = row_count // CTOK
    rank = lax.axis_index("tensor").astype(jnp.int32)
    place = lax.axis_index("cand").astype(jnp.int32)
    ranks = jnp.stack([rank, rank ^ 1, rank ^ 2, rank ^ 3])

    wide = tokens.astype(jnp.float32)
    scaled = (wide * pre_gain.astype(jnp.float32)).astype(jnp.bfloat16)
    bounds = [0]
    for share in TOKEN_CHUNKS:
        bounds.append(bounds[-1] + row_count * share // sum(TOKEN_CHUNKS))
    spans = [slice(a, b) for a, b in zip(bounds[:-1], bounds[1:])]

    blocks = []
    for c, span in enumerate(spans):
        own = scaled[span]
        if c == 1:
            own, square_sum = lax.optimization_barrier((own, square_sum))
        if c > 1:
            own, _ = lax.optimization_barrier((own, blocks[c - 2][2]))
        far = swap(own, 2)
        if c == 0:
            squares = jnp.sum(wide * wide, axis=1)
            squares, own = lax.optimization_barrier((squares, own))
            square_sum = sum_over_tensor(squares)
        blocks.append([own, swap(own, 1), far])
    inverse = lax.rsqrt(square_sum / model_width + epsilon)[:, None]

    mark = blocks[0][0][:16, :HEAD]
    key_values = []
    for c, span in enumerate(spans):
        if c in (1,):
            blocks[c][2], mark = lax.optimization_barrier((blocks[c][2], mark))
        blocks[c].append(swap(blocks[c][2], 1))
        if c:
            blocks[c][0], key_values[-1] = lax.optimization_barrier((blocks[c][0], key_values[-1]))
        projected, mark = project(ranks, mark, [blocks[c]], inverse[span], [w_key, w_value])
        key_values.append(projected)
    def outer(parts):
        return [lax.ppermute(x, "cand", [(0, 1), (1, 0), (2, 3), (3, 2)]) for x in parts]

    inner_pairs = [(0, 4), (4, 0), (3, 7), (7, 3), (1, 2), (2, 1), (5, 6), (6, 5)]

    def inner(parts):
        return [lax.ppermute(x, ("groups", "cand"), inner_pairs) for x in parts]

    outer_1 = outer(key_values)
    inner_1 = inner(key_values)
    outer_2 = outer(inner_1)
    inner_2 = inner(outer_1)
    outer_3 = outer(inner_2)
    at_end = (place == 0) | (place == CAND_AXIS - 1)

    def joined(parts, others):
        return jnp.where(at_end, jnp.concatenate(parts, axis=1), jnp.concatenate(others, axis=1))

    slots = [
        jnp.concatenate(key_values, axis=1),
        jnp.concatenate(outer_1, axis=1),
        joined(outer_2, inner_1),
    ]
    last_slot = joined(outer_3, inner_2)
    high = place >= 2
    shards = [
        place,
        place ^ 1,
        jnp.where(high, 1, 2),
        jnp.where(high, 0, 3),
    ]
    key_cand = jnp.concatenate(
        [s * cand_local + jnp.arange(cand_local, dtype=jnp.int32) for s in shards]
    )
    bias = bias_rows(cand_lengths, pair_mask, place * cand_local, cand_local, key_cand)
    queries, _ = project(ranks, blocks[0][0][:16, :HEAD], blocks, inverse, [w_query])
    seen = 3 * row_count
    state = attention(bias[:, :seen], queries, slots, ends=False)
    state, last_slot = lax.optimization_barrier((state, last_slot))

    gain_wide = post_gain.astype(jnp.float32)
    other_core = jnp.stack([rank ^ 3, rank ^ 1])
    this_core = jnp.stack([rank ^ 2, rank])
    step = row_count // OUTPUT_CHUNKS
    cands = step // CTOK
    pending = []
    for c in range(OUTPUT_CHUNKS):
        span = slice(c * step, (c + 1) * step)
        if c:
            last_slot, far = lax.optimization_barrier((last_slot, pending[-1][2]))
            pending[-1] = (*pending[-1][:2], far)
        rows = attention(
            bias[c * cands : (c + 1) * cands, seen:],
            queries[:, span],
            [last_slot],
            state=[x[span] for x in state],
        )
        away = swap(output_blocks(other_core, rows, w_out, features), 1)
        home = output_blocks(this_core, rows, w_out, features)
        far = (home[0].astype(jnp.float32) + away[0].astype(jnp.float32)).astype(jnp.bfloat16)
        pending.append((home[1], away[1], far))
    pending = [(home, away, swap(far, 2)) for home, away, far in pending]
    updates = []
    for home, away, far in pending:
        near = home.astype(jnp.float32) + away.astype(jnp.float32)
        mixed = near + far.astype(jnp.float32)
        mixed_sq = sum_over_tensor(jnp.sum(mixed * mixed, axis=1))
        inverse_post = lax.rsqrt(mixed_sq / model_width + epsilon)
        updates.append((mixed * inverse_post[:, None] * gain_wide).astype(jnp.bfloat16))
    return jnp.concatenate(updates, axis=0)


def per_device(
    tokens, pre_gain, w_query, w_key, w_value, w_out, post_gain, cand_lengths, pair_mask
):
    row_count = tokens.shape[0]
    model_width, query_width = w_query.shape
    kv_width = w_key.shape[1]
    weights_all = jnp.concatenate([w_query, w_key, w_value], axis=1)
    wide = tokens.astype(jnp.float32)
    square_sum = lax.psum(jnp.sum(wide * wide, axis=1), "tensor")
    scaled = (wide * pre_gain.astype(jnp.float32)).astype(jnp.bfloat16)
    scaled = lax.all_gather(scaled, "tensor", axis=1, tiled=True)
    inverse = lax.rsqrt(square_sum / model_width + epsilon)
    projected = jnp.dot(scaled, weights_all, preferred_element_type=jnp.float32)
    projected = (projected * inverse[:, None]).astype(jnp.bfloat16)
    keys = projected[:, query_width : query_width + kv_width]
    values = projected[:, query_width + kv_width :]
    cand_local = row_count // CTOK
    first_cand = lax.axis_index("cand").astype(jnp.int32) * cand_local
    key_cand = jnp.arange(pair_mask.shape[1], dtype=jnp.int32)
    bias = bias_rows(cand_lengths, pair_mask, first_cand, cand_local, key_cand)
    gathered = lax.all_gather(jnp.stack([keys, values]), "cand", axis=1, tiled=True)
    attended = attention(bias, projected[None, :, :query_width], [gathered])
    partial = jnp.dot(attended, w_out, preferred_element_type=jnp.float32).astype(jnp.bfloat16)
    mixed = lax.psum_scatter(partial.T, "tensor", scatter_dimension=0, tiled=True)
    mixed = mixed.astype(jnp.float32).T
    mixed_sq = lax.psum(jnp.sum(mixed * mixed, axis=1), "tensor")
    inverse_post = lax.rsqrt(mixed_sq / model_width + epsilon)
    return (mixed * inverse_post[:, None] * post_gain.astype(jnp.float32)).astype(jnp.bfloat16)


def solution(mesh):
    small = mesh.shape["tensor"] == 4 and mesh.shape["cand"] == CAND_AXIS
    small = small and mesh.shape["groups"] == 2
    return jax.shard_map(
        per_device_4x4 if small else per_device,
        mesh=mesh,
        in_specs=(
            P(("groups", "cand"), "tensor"),
            P(None, "tensor"),
            P(None, "tensor"),
            P(None, "tensor"),
            P(None, "tensor"),
            P("tensor", None),
            P(None, "tensor"),
            P("groups"),
            P("groups", None),
        ),
        out_specs=P(("groups", "cand"), "tensor"),
        check_vma=False,
    )
```

```python
import functools
import math

import jax
import jax.numpy as jnp
from jax import lax
from jax.experimental import pallas as pl
from jax.experimental.pallas import tpu as pltpu
from jax.sharding import PartitionSpec as P

HEADS = 32
KV_HEADS = 16
HEAD = 128
CTOK = 128
GROUP = HEADS // KV_HEADS
MASKED = -1e30
EXP2_SCALE = HEAD ** (-0.5) * math.log2(math.e)

epsilon = 1e-06


def bias_rows(cand_lengths, pair_mask, first_cand, cand_local, key_cand):
    allow_rows = lax.dynamic_slice_in_dim(pair_mask, first_cand, cand_local, 0)
    everyone = jnp.arange(pair_mask.shape[1], dtype=jnp.int32)
    one_hot = (everyone[:, None] == key_cand[None, :]).astype(jnp.float32)
    own = first_cand + jnp.arange(cand_local, dtype=jnp.int32)
    allowed = jnp.dot(allow_rows.astype(jnp.float32), one_hot) > 0.5
    allowed = allowed | (own[:, None] == key_cand[None, :])
    lengths = jnp.dot(cand_lengths.astype(jnp.float32)[None, :], one_hot)
    position = jnp.arange(CTOK, dtype=jnp.int32).astype(jnp.float32)
    inside = position[None, :] < lengths[0][:, None]
    usable = allowed[:, :, None] & inside[None]
    return jnp.where(usable, 0.0, MASKED).reshape(cand_local, key_cand.shape[0] * CTOK)


LONG = pl.CostEstimate(flops=10**10, transcendentals=0, bytes_accessed=10**6)
SHORT = pl.CostEstimate(flops=1, transcendentals=0, bytes_accessed=1)


def project_body(rank_ref, inverse_ref, *refs, chunks):
    x_refs = refs[: 4 * chunks]
    w_refs = refs[4 * chunks : -1]
    out_ref = refs[-1]
    features = x_refs[0].shape[1]
    start = 0
    for c in range(chunks):
        span = slice(start, start + x_refs[4 * c].shape[0])
        start = span.stop
        for i, w_ref in enumerate(w_refs):
            total = None
            for k in range(4):
                rows = pl.ds(pl.multiple_of(rank_ref[k] * features, HEAD), features)
                part = jnp.dot(
                    x_refs[4 * c + k][...], w_ref[rows, :], preferred_element_type=jnp.float32
                )
                total = part if total is None else total + part
            out_ref[i, span] = (total * inverse_ref[span]).astype(jnp.bfloat16)


def project(ranks, chunks, inverse, weights):
    vmem = pl.BlockSpec(memory_space=pltpu.VMEM)
    blocks = [x for chunk in chunks for x in chunk]
    return pl.pallas_call(
        functools.partial(project_body, chunks=len(chunks)),
        in_specs=[pl.BlockSpec(memory_space=pltpu.SMEM)]
        + [vmem] * (1 + len(blocks) + len(weights)),
        out_specs=vmem,
        out_shape=jax.ShapeDtypeStruct(
            (len(weights), inverse.shape[0], weights[0].shape[1]), jnp.bfloat16
        ),
        compiler_params=pltpu.CompilerParams(vmem_limit_bytes=24 * 2**20),
        cost_estimate=LONG,
        name="project",
    )(ranks, inverse, *blocks, *weights)


def scaled_scores(q, k, bias):
    scores = lax.dot_general(q, k, (((1,), (1,)), ((), ())), preferred_element_type=jnp.float32)
    return scores * EXP2_SCALE + bias


def attention_body(bias_ref, q_ref, *refs, slots, begun, ends):
    kv_refs = refs[: 2 * slots]
    state_refs = refs[2 * slots : 2 * slots + (2 if begun else 0)]
    out_refs = refs[2 * slots + len(state_refs) :]
    rows = q_ref.shape[1]
    for c in range(rows // CTOK):
        here = slice(c * CTOK, (c + 1) * CTOK)

        def stacked(ref):
            return jnp.concatenate(
                [ref[here, g * HEAD : (g + 1) * HEAD] for g in range(GROUP)], axis=0
            )

        q = stacked(q_ref.at[0])
        scores = []
        start = 0
        for s in range(slots):
            k = kv_refs[2 * s][0]
            scores.append(scaled_scores(q, k, bias_ref[c : c + 1, start : start + k.shape[0]]))
            start += k.shape[0]
        top = functools.reduce(jnp.maximum, [jnp.max(s, axis=1, keepdims=True) for s in scores])
        denominator = None
        numerator = None
        if begun:
            half = HEAD // GROUP
            old = jnp.concatenate(
                [state_refs[1][here, g * half : g * half + 1] for g in range(GROUP)], axis=0
            )
            top = jnp.maximum(old, top)
            denominator = jnp.exp2(old - top)
            numerator = stacked(state_refs[0]) * denominator
        for s in range(slots):
            p = jnp.exp2(scores[s] - top)
            d = jnp.sum(p, axis=1, keepdims=True)
            n = jnp.dot(
                p.astype(jnp.bfloat16), kv_refs[2 * s + 1][0], preferred_element_type=jnp.float32
            )
            denominator = d if denominator is None else denominator + d
            numerator = n if numerator is None else numerator + n
        out = numerator / denominator
        if ends:
            out = out.astype(jnp.bfloat16)
        for g in range(GROUP):
            out_refs[0][here, g * HEAD : (g + 1) * HEAD] = out[g * CTOK : (g + 1) * CTOK]
        if not ends:
            level = top + jnp.log2(denominator)
            half = HEAD // GROUP
            for g in range(GROUP):
                out_refs[1][here, g * half : (g + 1) * half] = jnp.broadcast_to(
                    level[g * CTOK : (g + 1) * CTOK], (CTOK, half)
                )


def attention(bias, queries, slots, state=(), ends=True):
    _, rows, width = queries.shape
    heads = width // (GROUP * HEAD)
    own = pl.BlockSpec((rows, GROUP * HEAD), lambda h: (0, h))
    level = pl.BlockSpec((rows, HEAD), lambda h: (0, h))
    in_specs = [
        pl.BlockSpec(bias.shape, lambda h: (0, 0)),
        pl.BlockSpec((1, rows, GROUP * HEAD), lambda h: (0, 0, h)),
    ]
    operands = []
    for kv in slots:
        for i in range(2):
            in_specs.append(pl.BlockSpec((1, kv.shape[1], HEAD), lambda h, i=i: (i, 0, h)))
            operands.append(kv)
    if ends:
        out_specs, out_shape = own, jax.ShapeDtypeStruct((rows, width), jnp.bfloat16)
    else:
        out_specs = (own, level)
        out_shape = (
            jax.ShapeDtypeStruct((rows, width), jnp.float32),
            jax.ShapeDtypeStruct((rows, heads * HEAD), jnp.float32),
        )
    return pl.pallas_call(
        functools.partial(attention_body, slots=len(slots), begun=len(state) > 0, ends=ends),
        grid=(heads,),
        in_specs=in_specs + ([own, level] if state else []),
        out_specs=out_specs,
        out_shape=out_shape,
        compiler_params=pltpu.CompilerParams(vmem_limit_bytes=20 * 2**20),
        cost_estimate=LONG,
        name="attention",
    )(bias, queries, *operands, *state)


def output_body(block_ref, x_ref, w_ref, out_ref):
    width = out_ref.shape[2]
    for b in range(out_ref.shape[0]):
        w = w_ref[:, pl.ds(pl.multiple_of(block_ref[b] * width, HEAD), width)]
        out_ref[b] = jnp.dot(x_ref[...], w, preferred_element_type=jnp.float32).astype(jnp.bfloat16)


def output_blocks(block_ids, attended, w_out, features):
    rows = attended.shape[0]
    return pl.pallas_call(
        output_body,
        in_specs=[
            pl.BlockSpec(memory_space=pltpu.SMEM),
            pl.BlockSpec(memory_space=pltpu.VMEM),
            pl.BlockSpec(memory_space=pltpu.VMEM),
        ],
        out_specs=pl.BlockSpec(memory_space=pltpu.VMEM),
        out_shape=jax.ShapeDtypeStruct((block_ids.shape[0], rows, features), jnp.bfloat16),
        compiler_params=pltpu.CompilerParams(vmem_limit_bytes=24 * 2**20),
        cost_estimate=LONG,
        name="output",
    )(block_ids, attended, w_out)


def swap(x, bit):
    return lax.ppermute(x, "tensor", [(t, t ^ bit) for t in range(4)])


def sum_over_tensor(x):
    return x + swap(x, 1) + (swap(x, 2) + swap(x, 3))


TOKEN_CHUNKS = (1, 1, 2, 4)
OUTPUT_CHUNKS = 2
CAND_AXIS = 4


def per_device_4x4(
    tokens, pre_gain, w_query, w_key, w_value, w_out, post_gain, cand_lengths, pair_mask
):
    row_count, features = tokens.shape
    model_width = w_query.shape[0]
    cand_local = row_count // CTOK
    rank = lax.axis_index("tensor").astype(jnp.int32)
    place = lax.axis_index("cand").astype(jnp.int32)
    ranks = jnp.stack([rank, rank ^ 1, rank ^ 2, rank ^ 3])

    wide = tokens.astype(jnp.float32)
    scaled = (wide * pre_gain.astype(jnp.float32)).astype(jnp.bfloat16)
    bounds = [0]
    for share in TOKEN_CHUNKS:
        bounds.append(bounds[-1] + row_count * share // sum(TOKEN_CHUNKS))
    spans = [slice(a, b) for a, b in zip(bounds[:-1], bounds[1:])]

    blocks = []
    for c, span in enumerate(spans):
        own = scaled[span]
        if c == 1:
            own, square_sum = lax.optimization_barrier((own, square_sum))
        if c > 1:
            own, _ = lax.optimization_barrier((own, blocks[c - 2][2]))
        far = swap(own, 2)
        if c == 0:
            squares = jnp.sum(wide * wide, axis=1)
            squares, own = lax.optimization_barrier((squares, own))
            square_sum = sum_over_tensor(squares)
        blocks.append([own, swap(own, 1), far, swap(far, 1)])
    inverse = lax.rsqrt(square_sum / model_width + epsilon)[:, None]

    key_values = []
    for c, span in enumerate(spans):
        if c:
            blocks[c][0], key_values[-1] = lax.optimization_barrier((blocks[c][0], key_values[-1]))
        key_values.append(project(ranks, [blocks[c]], inverse[span], [w_key, w_value]))
    def outer(parts):
        return [lax.ppermute(x, "cand", [(0, 1), (1, 0), (2, 3), (3, 2)]) for x in parts]

    inner_pairs = [(0, 4), (4, 0), (3, 7), (7, 3), (1, 2), (2, 1), (5, 6), (6, 5)]

    def inner(parts):
        return [lax.ppermute(x, ("groups", "cand"), inner_pairs) for x in parts]

    outer_1 = outer(key_values)
    inner_1 = inner(key_values)
    outer_2 = outer(inner_1)
    inner_2 = inner(outer_1)
    outer_3 = outer(inner_2)
    at_end = (place == 0) | (place == CAND_AXIS - 1)

    def joined(parts, others):
        return jnp.where(at_end, jnp.concatenate(parts, axis=1), jnp.concatenate(others, axis=1))

    slots = [
        jnp.concatenate(key_values, axis=1),
        jnp.concatenate(outer_1, axis=1),
        joined(outer_2, inner_1),
    ]
    last_slot = joined(outer_3, inner_2)
    high = place >= 2
    shards = [
        place,
        place ^ 1,
        jnp.where(high, 1, 2),
        jnp.where(high, 0, 3),
    ]
    key_cand = jnp.concatenate(
        [s * cand_local + jnp.arange(cand_local, dtype=jnp.int32) for s in shards]
    )
    bias = bias_rows(cand_lengths, pair_mask, place * cand_local, cand_local, key_cand)
    queries = project(ranks, blocks, inverse, [w_query])
    seen = 3 * row_count
    state = attention(bias[:, :seen], queries, slots, ends=False)
    state, last_slot = lax.optimization_barrier((state, last_slot))

    gain_wide = post_gain.astype(jnp.float32)
    other_core = jnp.stack([rank ^ 3, rank ^ 1])
    this_core = jnp.stack([rank ^ 2, rank])
    step = row_count // OUTPUT_CHUNKS
    cands = step // CTOK
    pending = []
    for c in range(OUTPUT_CHUNKS):
        span = slice(c * step, (c + 1) * step)
        if c:
            last_slot, far = lax.optimization_barrier((last_slot, pending[-1][2]))
            pending[-1] = (*pending[-1][:2], far)
        rows = attention(
            bias[c * cands : (c + 1) * cands, seen:],
            queries[:, span],
            [last_slot],
            state=[x[span] for x in state],
        )
        away = swap(output_blocks(other_core, rows, w_out, features), 1)
        home = output_blocks(this_core, rows, w_out, features)
        far = (home[0].astype(jnp.float32) + away[0].astype(jnp.float32)).astype(jnp.bfloat16)
        pending.append((home[1], away[1], far))
    pending = [(home, away, swap(far, 2)) for home, away, far in pending]
    updates = []
    for home, away, far in pending:
        near = home.astype(jnp.float32) + away.astype(jnp.float32)
        mixed = near + far.astype(jnp.float32)
        mixed_sq = sum_over_tensor(jnp.sum(mixed * mixed, axis=1))
        inverse_post = lax.rsqrt(mixed_sq / model_width + epsilon)
        updates.append((mixed * inverse_post[:, None] * gain_wide).astype(jnp.bfloat16))
    return jnp.concatenate(updates, axis=0)


def per_device(
    tokens, pre_gain, w_query, w_key, w_value, w_out, post_gain, cand_lengths, pair_mask
):
    row_count = tokens.shape[0]
    model_width, query_width = w_query.shape
    kv_width = w_key.shape[1]
    weights_all = jnp.concatenate([w_query, w_key, w_value], axis=1)
    wide = tokens.astype(jnp.float32)
    square_sum = lax.psum(jnp.sum(wide * wide, axis=1), "tensor")
    scaled = (wide * pre_gain.astype(jnp.float32)).astype(jnp.bfloat16)
    scaled = lax.all_gather(scaled, "tensor", axis=1, tiled=True)
    inverse = lax.rsqrt(square_sum / model_width + epsilon)
    projected = jnp.dot(scaled, weights_all, preferred_element_type=jnp.float32)
    projected = (projected * inverse[:, None]).astype(jnp.bfloat16)
    keys = projected[:, query_width : query_width + kv_width]
    values = projected[:, query_width + kv_width :]
    cand_local = row_count // CTOK
    first_cand = lax.axis_index("cand").astype(jnp.int32) * cand_local
    key_cand = jnp.arange(pair_mask.shape[1], dtype=jnp.int32)
    bias = bias_rows(cand_lengths, pair_mask, first_cand, cand_local, key_cand)
    gathered = lax.all_gather(jnp.stack([keys, values]), "cand", axis=1, tiled=True)
    attended = attention(bias, projected[None, :, :query_width], [gathered])
    partial = jnp.dot(attended, w_out, preferred_element_type=jnp.float32).astype(jnp.bfloat16)
    mixed = lax.psum_scatter(partial.T, "tensor", scatter_dimension=0, tiled=True)
    mixed = mixed.astype(jnp.float32).T
    mixed_sq = lax.psum(jnp.sum(mixed * mixed, axis=1), "tensor")
    inverse_post = lax.rsqrt(mixed_sq / model_width + epsilon)
    return (mixed * inverse_post[:, None] * post_gain.astype(jnp.float32)).astype(jnp.bfloat16)


def solution(mesh):
    small = mesh.shape["tensor"] == 4 and mesh.shape["cand"] == CAND_AXIS
    small = small and mesh.shape["groups"] == 2
    return jax.shard_map(
        per_device_4x4 if small else per_device,
        mesh=mesh,
        in_specs=(
            P(("groups", "cand"), "tensor"),
            P(None, "tensor"),
            P(None, "tensor"),
            P(None, "tensor"),
            P(None, "tensor"),
            P("tensor", None),
            P(None, "tensor"),
            P("groups"),
            P("groups", None),
        ),
        out_specs=P(("groups", "cand"), "tensor"),
        check_vma=False,
    )
```
